32 devices in a mesh: dp: 4 (over y, core), space: 8 (over z, x).
Axes of the slice: x: 2, y: 2, z: 4, core: 2. Of those that a mesh axis runs over, the one named last changes fastest.
Arguments:
- activations: bfloat16 [2, 4, 8, 16, 32, 768], P(None, 'dp', None, 'space'), may hold values from -60 to 60
- out_grads: bfloat16 [2, 4, 8, 16, 32, 768], P(None, 'dp', None, 'space'), may hold values from -6 to 6
- omega: bfloat16 [768, 128], replicated, may hold values from -0.21875 to 0.21875
Outputs:
- basis: float32 [2, 20736, 128], P(None, ('dp', 'space'))
The draws below stay inside these ranges and needn't reach their ends.
All inputs are finite; a program needn't handle non-finite values.
Results may differ from the reference program's by a relative error of at most 0.0033.
Values may be sent and summed in bfloat16 or wider, within the bound.
No kernel may reach another device: no remote copies, remote signals or barrier semaphores. Data moves between devices by JAX's collectives and lax.ppermute only.
A program may use at most 128 MiB of HBM per device.

```python
import math
import jax
import jax.numpy as jnp
from jax import lax

C = 768
RANK = 128
LAYERS = 2
FRAMES = 8
WCOLS = 32
BATCH = 4
HEIGHT = 16
KROWS = 20736


def draw_activations(key, part):
    scale_key, base_key = jax.random.split(key, 2)
    shape = (LAYERS, BATCH, FRAMES, HEIGHT, WCOLS, C)
    scales = jnp.exp(jax.random.uniform(scale_key, (LAYERS, 1, 1, 1, 1, C), jnp.float32, 0.0, math.log(10.0)))
    base = jnp.clip(jax.random.normal(base_key, shape, jnp.float32), -6.0, 6.0)
    return (base * scales).astype(jnp.bfloat16)


def steps_of(own_key, shape, shards, smallest, largest):
    loudness = 1.0
    for axis_at, parts in shards:
        draws = jax.random.uniform(jax.random.fold_in(jax.random.fold_in(own_key, 6), axis_at), (parts,), jnp.float32, smallest / len(shards), largest / len(shards))
        loudness = loudness * jnp.repeat(jnp.exp(draws), shape[axis_at] // parts).reshape((-1,) + (1,) * (len(shape) - 1 - axis_at))
    return loudness


def normal_values(key, dims, scale, reach, shards=(), held_as=jnp.bfloat16):
    values = jax.random.normal(key, dims, jnp.float32) * scale
    if len(shards) > 0:
        values = steps_of(key, dims, shards, -0.22, 0.18) * values
    return jnp.clip(values, min=-reach, max=reach).astype(held_as)


def setup_inputs(seed: int = 0) -> dict:
    key_of = jax.random.split(jax.random.key(seed), 4)
    return {
        "activations": draw_activations(jax.random.fold_in(key_of[3], 71), 0),
        "out_grads": normal_values(key_of[1], (LAYERS, BATCH, FRAMES, HEIGHT, WCOLS, C), 1.0, 6.0, ((1, 4), (3, 8))),
        "omega": normal_values(key_of[2], (C, RANK), C ** -0.5, 0.21875),
    }


def reference(activations, out_grads, omega):
    results = []
    for layer in range(LAYERS):
        grads_flat = out_grads[layer].reshape(-1, C)
        sketched = jnp.dot(grads_flat.astype(jnp.float32), omega.astype(jnp.float32), preferred_element_type=jnp.float32).astype(jnp.bfloat16)
        padded = jnp.pad(activations[layer], ((0, 0), (1, 1), (1, 1), (1, 1), (0, 0)))
        blocks = []
        for along_t in range(3):
            for along_h in range(3):
                for along_w in range(3):
                    window = padded[:, along_t:along_t + FRAMES, along_h:along_h + HEIGHT, along_w:along_w + WCOLS, :]
                    window = window.reshape(-1, C)
                    blocks.append(jnp.dot(window.T.astype(jnp.float32), sketched.astype(jnp.float32), preferred_element_type=jnp.float32))
        sketch = jnp.concatenate(blocks, axis=0)
        gram = jnp.dot(sketch.T, sketch, precision=lax.Precision.HIGHEST)
        lower = jnp.linalg.cholesky(gram)
        basis = jax.scipy.linalg.solve_triangular(lower, sketch.T, lower=True).T
        results.append(basis * math.sqrt(KROWS))
    return jnp.stack(results)
```

```python
import functools
import math

import jax
import jax.numpy as jnp
from jax import lax
from jax.experimental import pallas as pl
from jax.experimental.pallas import tpu as pltpu
from jax.sharding import PartitionSpec as P

AXES = ("dp", "space")
F32, BF16 = jnp.float32, jnp.bfloat16
HIGHEST = lax.Precision.HIGHEST


def swap(value, mask, total):
    return lax.ppermute(value, AXES, [(d, d ^ mask) for d in range(total)])


def halo(value, axis, dim):
    count, length = lax.axis_size(axis), value.shape[dim]
    up = [(i, i + 1) for i in range(count - 1)]
    before = lax.ppermute(lax.slice_in_dim(value, length - 1, length, axis=dim), axis, up)
    after = lax.ppermute(lax.slice_in_dim(value, 0, 1, axis=dim), axis, [(j, i) for i, j in up])
    return jnp.concatenate([before, value, after], axis=dim)


def product_kernel(frames, height, widths, rank, act_ref, sk_ref, out_ref, act_t, wide):
    step = pl.program_id(0)

    @pl.when(step == 0)
    def _():
        act_t[...] = act_ref[...].T
        zero = jnp.zeros((height + 2, widths, 3 * rank), BF16)
        wide[0] = zero
        wide[frames + 1] = zero
        rows = frames * (height + 2) * widths
        flat = sk_ref[...].astype(F32).reshape(rows, rank)
        at = lax.rem(lax.broadcasted_iota(jnp.int32, (rows, rank), 0), widths)
        later = jnp.where(at == widths - 1, 0.0, pltpu.roll(flat, rows - 1, 0))
        earlier = jnp.where(at == 0, 0.0, pltpu.roll(flat, 1, 0))
        shape = (frames, height + 2, widths, rank)
        wide[1 : frames + 1, :, :, 0:rank] = later.astype(BF16).reshape(shape)
        wide[1 : frames + 1, :, :, rank : 2 * rank] = sk_ref[...]
        wide[1 : frames + 1, :, :, 2 * rank :] = earlier.astype(BF16).reshape(shape)

    along_t, along_h = step // 3, lax.rem(step, 3)
    window = wide[pl.ds(2 - along_t, frames), pl.ds(2 - along_h, height)]
    window = window.reshape(frames * height * widths, 3 * rank)
    made = jnp.dot(act_t[...], window, preferred_element_type=F32)
    for c in range(3):
        out_ref[c] = made[:, c * rank : (c + 1) * rank]


def product(act, extended):
    frames, rows, widths, rank = extended.shape
    height, channels = rows - 2, act.shape[-1]
    positions = frames * height * widths
    return pl.pallas_call(
        functools.partial(product_kernel, frames, height, widths, rank),
        grid=(9,),
        in_specs=[
            pl.BlockSpec((positions, channels), lambda s: (0, 0)),
            pl.BlockSpec((frames, rows, widths, rank), lambda s: (0, 0, 0, 0)),
        ],
        out_specs=pl.BlockSpec((3, channels, rank), lambda s: (s, 0, 0)),
        out_shape=jax.ShapeDtypeStruct((27, channels, rank), F32),
        scratch_shapes=[
            pltpu.VMEM((channels, positions), BF16),
            pltpu.VMEM((frames + 2, rows, widths, 3 * rank), BF16),
        ],
        compiler_params=pltpu.CompilerParams(vmem_limit_bytes=40 * 2**20),
        cost_estimate=pl.CostEstimate(
            flops=2 * 27 * positions * channels * rank,
            bytes_accessed=27 * channels * rank * 4 + positions * channels * 2,
            transcendentals=0,
        ),
        name="product",
    )(act.reshape(positions, channels), extended)


def inverse_kernel(size, gram_ref, out_ref, work):
    eye = lax.broadcasted_iota(jnp.int32, (size, size), 0) == lax.broadcasted_iota(jnp.int32, (size, size), 1)
    work[:, :size] = gram_ref[...]
    work[:, size:] = eye.astype(F32)
    sub = lax.broadcasted_iota(jnp.int32, (8, 1), 0)
    for start in range(0, size, 8):
        rows = work[start : start + 8, :]
        cols = [jnp.broadcast_to(rows[:, start + r : start + r + 1], (8, size)) for r in range(8)]
        for r in range(8):
            scale = lax.rsqrt(cols[r][r : r + 1, :])
            below = jnp.where(sub > r, cols[r] * scale, 0.0)
            for c in range(r + 1, 8):
                cols[c] = cols[c] - below * (cols[c][r : r + 1, :] * scale)
            both = jnp.concatenate([scale, scale], axis=1)
            row = rows[r : r + 1, :] * both
            rows = jnp.where(sub == r, row, rows - jnp.concatenate([below, below], axis=1) * row)
        out_ref[start : start + 8, :] = rows[:, size:]
        if start + 8 < size:
            left = rows[:, start + 8 : size] if (start + 8) % size == 0 else rows[:, :size]
            update = lax.dot_general(
                left, rows, (((0,), (0,)), ((), ())), precision=HIGHEST, preferred_element_type=F32
            )
            work[start + 8 :, :] = work[start + 8 :, :] - update[start + 8 :, :]


def inverse_of_factor(gram):
    size = gram.shape[-1]
    return pl.pallas_call(
        functools.partial(inverse_kernel, size),
        out_shape=jax.ShapeDtypeStruct((size, size), F32),
        scratch_shapes=[pltpu.VMEM((size, 2 * size), F32)],
        name="inverse",
    )(gram)


def pick(value, index, axis):
    return lax.dynamic_index_in_dim(value, index, axis, keepdims=False)


def halve(value, axis, own, mask, total):
    sent = pick(value, 1 - own, axis).astype(BF16)
    return pick(value, own, axis) + swap(sent, mask, total).astype(F32)


def scatter_layer(partial, bits, total):
    rank = partial.shape[-1]
    rows = partial.shape[0] * partial.shape[1] // total
    count = len(bits)
    core_at = count - 1 - (lax.axis_size("space").bit_length() - 1)
    view = partial.reshape((2,) * count + (rows, rank))
    masks = [1 << (count - 1 - i) for i in range(count)]
    if count == 5 and core_at == 1:
        y, _, zh, zl, x = bits
        my, mc, mzh, mzl, mx = masks
        view = halve(view, 1, bits[1], mc, total)
        one, two = view[:, 0], view[:, 1]
        one = halve(one, 2, x, mx, total)
        two = halve(two, 0, y, my, total)
        one = halve(one, 0, y, my, total)
        two = halve(two, 1, x, mx, total)
        z = 2 * zh + zl
        both = jnp.stack([one, two]).reshape(4, rows, rank)
        got = [swap(pick(both, z ^ m, 0).astype(BF16), m * mzl, total) for m in (1, 2, 3)]
        return pick(both, z, 0) + (got[0].astype(F32) + got[1].astype(F32) + got[2].astype(F32))
    order = [core_at] + [i for i in range(count) if i != core_at]
    left = list(range(count))
    for i in order:
        view = halve(view, left.index(i), bits[i], masks[i], total)
        left.remove(i)
    return view


def shards(activations, out_grads, omega):
    layer_count, clips, frames, height, widths, channels = activations.shape
    rank = omega.shape[1]
    total = lax.axis_size("dp") * lax.axis_size("space")
    count = total.bit_length() - 1
    me = lax.axis_index("dp") * lax.axis_size("space") + lax.axis_index("space")
    bits = [(me >> (count - 1 - i)) & 1 for i in range(count)]
    core_mask = lax.axis_size("space")
    core = lax.axis_index("dp") & 1

    sketched = jnp.dot(out_grads.reshape(-1, channels), omega, preferred_element_type=F32).astype(BF16)
    sketched = sketched.reshape(layer_count, frames, height, widths, rank)
    extended = halo(sketched, "space", 2)
    blocks = []
    for layer in range(layer_count):
        partial = product(activations[layer], extended[layer])
        blocks.append(scatter_layer(partial, bits, total))
    rows = jnp.stack(blocks)
    gram = jnp.einsum("lnr,lns->lrs", rows, rows, precision=HIGHEST)
    mine = pick(gram, core, 0) + swap(pick(gram, 1 - core, 0), core_mask, total)
    for i in range(count):
        mask = 1 << i
        if mask != core_mask:
            mine = mine + swap(mine, mask, total)
    inverse = inverse_of_factor(mine)
    other = swap(inverse, core_mask, total)
    inverses = [jnp.where(core == layer, inverse, other) for layer in range(2)]
    scale = math.sqrt(27 * channels)
    basis = [jnp.dot(rows[i], inverses[i].T, precision=HIGHEST) * scale for i in range(2)]
    return jnp.stack(basis)


def solution(mesh):
    return jax.shard_map(
        shards,
        mesh=mesh,
        in_specs=(
            P(None, "dp", None, "space", None, None),
            P(None, "dp", None, "space", None, None),
            P(),
        ),
        out_specs=P(None, ("dp", "space"), None),
        check_vma=False,
    )
```

```python
import functools
import math

import jax
import jax.numpy as jnp
import numpy as np
from jax import lax
from jax.experimental import pallas as pl
from jax.experimental.pallas import tpu as pltpu
from jax.sharding import PartitionSpec as P

AXES = ("dp", "space")
F32, BF16 = jnp.float32, jnp.bfloat16
HIGHEST = lax.Precision.HIGHEST


def swap(value, mask, total):
    return lax.ppermute(value, AXES, [(d, d ^ mask) for d in range(total)])


def halo(value, axis, dim):
    count, length = lax.axis_size(axis), value.shape[dim]
    up = [(i, i + 1) for i in range(count - 1)]
    before = lax.ppermute(lax.slice_in_dim(value, length - 1, length, axis=dim), axis, up)
    after = lax.ppermute(lax.slice_in_dim(value, 0, 1, axis=dim), axis, [(j, i) for i, j in up])
    return jnp.concatenate([before, value, after], axis=dim)


def product_kernel(frames, height, widths, rank, act_ref, sk_ref, out_ref, act_t, wide):
    step = pl.program_id(0)

    @pl.when(step == 0)
    def _():
        act_t[...] = act_ref[...].T
        zero = jnp.zeros((height + 2, widths, 3 * rank), BF16)
        wide[0] = zero
        wide[frames + 1] = zero
        rows = frames * (height + 2) * widths
        flat = sk_ref[...].astype(F32).reshape(rows, rank)
        at = lax.rem(lax.broadcasted_iota(jnp.int32, (rows, rank), 0), widths)
        later = jnp.where(at == widths - 1, 0.0, pltpu.roll(flat, rows - 1, 0))
        earlier = jnp.where(at == 0, 0.0, pltpu.roll(flat, 1, 0))
        shape = (frames, height + 2, widths, rank)
        wide[1 : frames + 1, :, :, 0:rank] = later.astype(BF16).reshape(shape)
        wide[1 : frames + 1, :, :, rank : 2 * rank] = sk_ref[...]
        wide[1 : frames + 1, :, :, 2 * rank :] = earlier.astype(BF16).reshape(shape)

    along_t, along_h = step // 3, lax.rem(step, 3)
    window = wide[pl.ds(2 - along_t, frames), pl.ds(2 - along_h, height)]
    window = window.reshape(frames * height * widths, 3 * rank)
    made = jnp.dot(act_t[...], window, preferred_element_type=F32)
    for c in range(3):
        out_ref[c] = made[:, c * rank : (c + 1) * rank]


def product(act, extended):
    frames, rows, widths, rank = extended.shape
    height, channels = rows - 2, act.shape[-1]
    positions = frames * height * widths
    return pl.pallas_call(
        functools.partial(product_kernel, frames, height, widths, rank),
        grid=(9,),
        in_specs=[
            pl.BlockSpec((positions, channels), lambda s: (0, 0)),
            pl.BlockSpec((frames, rows, widths, rank), lambda s: (0, 0, 0, 0)),
        ],
        out_specs=pl.BlockSpec((3, channels, rank), lambda s: (s, 0, 0)),
        out_shape=jax.ShapeDtypeStruct((27, channels, rank), F32),
        scratch_shapes=[
            pltpu.VMEM((channels, positions), BF16),
            pltpu.VMEM((frames + 2, rows, widths, 3 * rank), BF16),
        ],
        compiler_params=pltpu.CompilerParams(vmem_limit_bytes=40 * 2**20),
        cost_estimate=pl.CostEstimate(
            flops=2 * 27 * positions * channels * rank,
            bytes_accessed=27 * channels * rank * 4 + positions * channels * 2,
            transcendentals=0,
        ),
        name="product",
    )(act.reshape(positions, channels), extended)


def inverse_kernel(size, gram_ref, out_ref, work):
    eye = lax.broadcasted_iota(jnp.int32, (size, size), 0) == lax.broadcasted_iota(jnp.int32, (size, size), 1)
    work[:, :size] = gram_ref[...]
    work[:, size:] = eye.astype(F32)
    sub = lax.broadcasted_iota(jnp.int32, (8, 1), 0)
    for start in range(0, size, 8):
        rows = work[start : start + 8, :]
        cols = [jnp.broadcast_to(rows[:, start + r : start + r + 1], (8, size)) for r in range(8)]
        for r in range(8):
            scale = lax.rsqrt(cols[r][r : r + 1, :])
            below = jnp.where(sub > r, cols[r] * scale, 0.0)
            for c in range(r + 1, 8):
                cols[c] = cols[c] - below * (cols[c][r : r + 1, :] * scale)
            both = jnp.concatenate([scale, scale], axis=1)
            row = rows[r : r + 1, :] * both
            rows = jnp.where(sub == r, row, rows - jnp.concatenate([below, below], axis=1) * row)
        out_ref[start : start + 8, :] = rows[:, size:]
        if start + 8 < size:
            left = rows[:, start + 8 : size] if (start + 8) % size == 0 else rows[:, :size]
            update = lax.dot_general(
                left, rows, (((0,), (0,)), ((), ())), precision=HIGHEST, preferred_element_type=F32
            )
            work[start + 8 :, :] = work[start + 8 :, :] - update[start + 8 :, :]


def inverse_of_factor(gram):
    size = gram.shape[-1]
    return pl.pallas_call(
        functools.partial(inverse_kernel, size),
        out_shape=jax.ShapeDtypeStruct((size, size), F32),
        scratch_shapes=[pltpu.VMEM((size, 2 * size), F32)],
        name="inverse",
    )(gram)


def pick(value, index, axis):
    return lax.dynamic_index_in_dim(value, index, axis, keepdims=False)


def halve(value, axis, own, mask, total):
    sent = pick(value, 1 - own, axis).astype(BF16)
    return pick(value, own, axis) + swap(sent, mask, total).astype(F32)


def scatter_layer(partial, bits, total):
    rank = partial.shape[-1]
    rows = partial.shape[0] * partial.shape[1] // total
    count = len(bits)
    core_at = count - 1 - (lax.axis_size("space").bit_length() - 1)
    view = partial.reshape((2,) * count + (rows, rank))
    masks = [1 << (count - 1 - i) for i in range(count)]
    if count == 5 and core_at == 1:
        y, _, zh, zl, x = bits
        my, mc, mzh, mzl, mx = masks
        view = halve(view, 1, bits[1], mc, total)
        one, two = view[:, 0], view[:, 1]
        one = halve(one, 2, x, mx, total)
        two = halve(two, 0, y, my, total)
        one = halve(one, 0, y, my, total)
        two = halve(two, 1, x, mx, total)
        z = 2 * zh + zl
        both = jnp.stack([one, two]).reshape(4, rows, rank)
        got = [swap(pick(both, z ^ m, 0).astype(BF16), m * mzl, total) for m in (1, 2, 3)]
        return pick(both, z, 0) + (got[0].astype(F32) + got[1].astype(F32) + got[2].astype(F32))
    order = [core_at] + [i for i in range(count) if i != core_at]
    left = list(range(count))
    for i in order:
        view = halve(view, left.index(i), bits[i], masks[i], total)
        left.remove(i)
    return view


def shards(activations, out_grads, omega):
    layer_count, clips, frames, height, widths, channels = activations.shape
    rank = omega.shape[1]
    total = lax.axis_size("dp") * lax.axis_size("space")
    count = total.bit_length() - 1
    me = lax.axis_index("dp") * lax.axis_size("space") + lax.axis_index("space")
    bits = [(me >> (count - 1 - i)) & 1 for i in range(count)]
    core_mask = lax.axis_size("space")
    core = lax.axis_index("dp") & 1

    sketched = jnp.dot(out_grads.reshape(-1, channels), omega, preferred_element_type=F32).astype(BF16)
    sketched = sketched.reshape(layer_count, frames, height, widths, rank)
    extended = halo(sketched, "space", 2)
    blocks = []
    for layer in range(layer_count):
        partial = product(activations[layer], extended[layer])
        blocks.append(scatter_layer(partial, bits, total))
    rows = jnp.stack(blocks)
    gram = jnp.einsum("lnr,lns->lrs", rows, rows, precision=HIGHEST)
    mine = pick(gram, core, 0) + swap(pick(gram, 1 - core, 0), core_mask, total)
    for i in range(count):
        mask = 1 << i
        if mask != core_mask:
            mine = mine + swap(mine, mask, total)
    inverse = inverse_of_factor(mine)
    other = swap(inverse, core_mask, total)
    inverses = [jnp.where(core == layer, inverse, other) for layer in range(2)]
    scale = math.sqrt(27 * channels)
    basis = [jnp.dot(rows[i], inverses[i].T, precision=HIGHEST) * scale for i in range(2)]
    return jnp.stack(basis)


DP_BITS, SPACE_BITS = 2, 3
UNITS = 28


@functools.lru_cache
def unit_tables():
    table = np.zeros((32, 4 * UNITS + 32 + 27), np.int32)
    for device in range(32):
        y, core, z, x = device >> 4, (device >> 3) & 1, (device >> 1) & 3, device & 1
        quarter = 2 * y + x
        first = 16 * core + 4 * quarter
        def units_for(target):
            return [4 * k + s for k in range(27) for s in range(4) if ((32 * k + first + s) // 54) % 4 == target]
        row = []
        for m in range(4):
            units = units_for(z ^ m)
            row += units + [108] * (UNITS - len(units))
        held = units_for(z)
        for m in range(4):
            for other in range(2):
                q = quarter ^ m
                target = ((q >> 1) << 4) | ((core ^ other) << 3) | (z << 1) | (q & 1)
                for s in range(4):
                    found = [p for p, n in enumerate(held) if n % 4 == s and (8 * (n - s) + first + s) // 27 == target]
                    row.append(found[0] if found else UNITS)
        for v in range(27):
            column = (27 * device + v) % 32
            row.append(16 * ((column // 16) ^ core) + 4 * (((column % 16) // 4) ^ quarter) + column % 4)
        table[device] = row
    return table


def turn_kernel(frames, chunk, half, where_ref, own_ref, got_ref, out_ref):
    at = pl.multiple_of(where_ref[0] * half, 128)
    for t in range(frames):
        rows = slice(chunk * t, chunk * (t + 1))
        block = jnp.concatenate([own_ref[rows, pl.ds(at, half)], got_ref[rows, :]], axis=0)
        out_ref[:, :, 2 * chunk * t : 2 * chunk * (t + 1)] = block.T.reshape(4, half // 4, 2 * chunk)


def turn(where, own, got, frames):
    positions, half = got.shape
    return pl.pallas_call(
        functools.partial(turn_kernel, frames, positions // frames, half),
        in_specs=[pl.BlockSpec(memory_space=pltpu.SMEM)] + [pl.BlockSpec(memory_space=pltpu.VMEM)] * 2,
        out_specs=pl.BlockSpec(memory_space=pltpu.VMEM),
        out_shape=jax.ShapeDtypeStruct((4, half // 4, 2 * positions), BF16),
        cost_estimate=pl.CostEstimate(flops=0, bytes_accessed=8 * positions * half, transcendentals=0),
        name="turn",
    )(where, own, got)


def plane_kernel(frames, widths, rank, where_ref, table_ref, act_ref, a1, a2, a3, own_ref, other_ref,
                 keep_ref, s1, s2, s3, lhs, wide, acc, units):
    x, quarter = where_ref[1], where_ref[2]
    each = act_ref.shape[1]
    depth = act_ref.shape[2]
    frame = depth // frames
    for m, ref in enumerate((act_ref, a1, a2, a3)):
        value = ref[quarter] if m == 0 else ref[...]
        zero = jnp.zeros((each, frame), BF16)
        lhs[m, 0:each, 0:frame] = zero
        lhs[m, 0:each, frame:] = value[:, : depth - frame]
        lhs[m, each : 2 * each, :] = value
        lhs[m, 2 * each :, : depth - frame] = value[:, frame:]
        lhs[m, 2 * each :, depth - frame :] = zero
    rows = frames * 3 * widths
    at = lax.rem(lax.broadcasted_iota(jnp.int32, (rows, rank), 0), widths)
    for side, ref in enumerate((own_ref, other_ref)):
        for m in range(4):
            piece = ref[m]
            to = pl.ds(3 * (x ^ (m & 1)), 3)
            flat = piece.astype(F32).reshape(rows, rank)
            later = jnp.where(at == widths - 1, 0.0, pltpu.roll(flat, rows - 1, 0))
            earlier = jnp.where(at == 0, 0.0, pltpu.roll(flat, 1, 0))
            wide[m >> 1, :, side, to, :, 0:rank] = later.astype(BF16).reshape(piece.shape)
            wide[m >> 1, :, side, to, :, rank : 2 * rank] = piece
            wide[m >> 1, :, side, to, :, 2 * rank :] = earlier.astype(BF16).reshape(piece.shape)

    blocks = each // 24
    units[27 * blocks] = jnp.zeros((24, rank), F32)

    @pl.loop(0, 3)
    def _(along_h):
        for m in range(4):
            window = wide[m >> 1, :, :, pl.ds(2 * (x ^ (m & 1)) + 2 - along_h, 2)]
            made = jnp.dot(lhs[m], window.reshape(depth, 3 * rank), preferred_element_type=F32)
            acc[...] = made if m == 0 else acc[...] + made
        for a in range(3):
            for c in range(3):
                part = acc[a * each : (a + 1) * each, c * rank : (c + 1) * rank]
                units[pl.ds((9 * a + 3 * along_h + c) * blocks, blocks)] = part.reshape(blocks, 24, rank)

    @pl.loop(0, UNITS)
    def _(p):
        keep_ref[p] = units[table_ref[p]]
        for m, ref in enumerate((s1, s2, s3)):
            ref[p] = units[table_ref[(m + 1) * UNITS + p]].astype(BF16)


def plane(where, table, act, got, own, other):
    frames, _, widths, rank = own.shape[1:]
    each, depth = act.shape[1:]
    vmem = pl.BlockSpec(memory_space=pltpu.VMEM)
    smem = pl.BlockSpec(memory_space=pltpu.SMEM)
    return pl.pallas_call(
        functools.partial(plane_kernel, frames, widths, rank),
        in_specs=[smem, smem] + [vmem] * 6,
        out_specs=[vmem] * 4,
        out_shape=[jax.ShapeDtypeStruct((UNITS, 24, rank), F32)]
        + [jax.ShapeDtypeStruct((UNITS, 24, rank), BF16)] * 3,
        scratch_shapes=[
            pltpu.VMEM((4, 3 * each, depth), BF16),
            pltpu.VMEM((2, frames, 2, 6, widths, 3 * rank), BF16),
            pltpu.VMEM((3 * each, 3 * rank), F32),
            pltpu.VMEM((27 * each // 24 + 1, 24, rank), F32),
        ],
        compiler_params=pltpu.CompilerParams(vmem_limit_bytes=30 * 2**20),
        cost_estimate=pl.CostEstimate(
            flops=2 * 27 * 4 * depth * each * rank, bytes_accessed=6 * 2**20, transcendentals=0
        ),
        name="plane",
    )(where, table, act, *got, own, other)


def gather_kernel(rank, table_ref, keep_ref, g1, g2, g3, gram_ref, p0, p1, p2, p3, rows):
    total = keep_ref[...] + (g1[...].astype(F32) + g2[...].astype(F32) + g3[...].astype(F32))
    rows[0:UNITS] = total
    rows[UNITS] = jnp.zeros((24, rank), F32)
    for m, ref in enumerate((p0, p1, p2, p3)):
        for other in range(2):
            for s in range(4):
                ref[other, s] = rows[table_ref[4 * UNITS + 8 * m + 4 * other + s]]
    flat = total.reshape(UNITS * 24, rank)
    gram_ref[...] = lax.dot_general(
        flat, flat, (((0,), (0,)), ((), ())), precision=HIGHEST, preferred_element_type=F32
    )


def gather(table, keep, got):
    rank = keep.shape[-1]
    vmem = pl.BlockSpec(memory_space=pltpu.VMEM)
    return pl.pallas_call(
        functools.partial(gather_kernel, rank),
        in_specs=[pl.BlockSpec(memory_space=pltpu.SMEM)] + [vmem] * 4,
        out_specs=[vmem] * 5,
        out_shape=[jax.ShapeDtypeStruct((rank, rank), F32)] + [jax.ShapeDtypeStruct((2, 4, 24, rank), F32)] * 4,
        scratch_shapes=[pltpu.VMEM((UNITS + 1, 24, rank), F32)],
        cost_estimate=pl.CostEstimate(flops=12 * UNITS * 24 * rank * rank, bytes_accessed=2**20, transcendentals=0),
        name="gather",
    )(table, keep, *got)


def basis_kernel(scale, where_ref, table_ref, own0, own1, other0, other1, mine_ref, theirs_ref, out_ref, rows):
    core = where_ref[0]
    for layer, refs in enumerate(((own0, other0), (own1, other1))):
        for v in range(27):
            n = table_ref[4 * UNITS + 32 + v]

            @pl.when(n < 16)
            def _():
                rows[24 * v : 24 * v + 24, :] = refs[0][n]

            @pl.when(n >= 16)
            def _():
                rows[24 * v : 24 * v + 24, :] = refs[1][n - 16]

        inverse = jnp.where(core == layer, mine_ref[...], theirs_ref[...])
        made = lax.dot_general(
            rows[...], inverse, (((1,), (1,)), ((), ())), precision=HIGHEST, preferred_element_type=F32
        )
        out_ref[layer] = made * scale


def basis_of(where, table, own, other, mine, theirs, scale):
    rank = mine.shape[0]
    vmem = pl.BlockSpec(memory_space=pltpu.VMEM)
    smem = pl.BlockSpec(memory_space=pltpu.SMEM)
    return pl.pallas_call(
        functools.partial(basis_kernel, scale),
        in_specs=[smem, smem] + [vmem] * 6,
        out_specs=vmem,
        out_shape=jax.ShapeDtypeStruct((2, 27 * 24, rank), F32),
        scratch_shapes=[pltpu.VMEM((27 * 24, rank), F32)],
        name="basis",
    )(where, table, *own, *other, mine, theirs)


def planes(activations, out_grads, omega):
    layer_count, _, frames, height, widths, channels = activations.shape
    rank = omega.shape[1]
    dp, space = lax.axis_index("dp"), lax.axis_index("space")
    core, x = dp & 1, space & 1
    quarter = 2 * (dp >> 1) + x
    me = 8 * dp + space
    move = functools.partial(swap, total=32)
    core_mask, chip_masks, z_masks = 8, (1, 16, 17), (2, 4, 6)
    where = jnp.stack([core, x, quarter]).astype(jnp.int32)
    table = lax.dynamic_index_in_dim(jnp.asarray(unit_tables()), me, 0, keepdims=False)
    positions, half = frames * height * widths, channels // 2

    acts = [activations[layer].reshape(positions, channels) for layer in range(2)]
    over = [lax.dynamic_slice_in_dim(a, (1 - core) * half, half, axis=1) for a in acts]
    over = [move(a, core_mask) for a in over]

    sketched = jnp.dot(out_grads.reshape(-1, channels), omega, preferred_element_type=F32).astype(BF16)
    sketched = sketched.reshape(layer_count, frames, height, widths, rank)
    edge = jnp.where(x == 1, sketched[:, :, height - 1], sketched[:, :, 0])
    pairs = [(i, i + 1) for i in range(1, 7, 2)]
    edge = lax.ppermute(edge, "space", pairs + [(j, i) for i, j in pairs])[:, :, None]
    pieces = jnp.where(
        x == 1, jnp.concatenate([sketched, edge], axis=2), jnp.concatenate([edge, sketched], axis=2)
    )

    grams, kept, sent = [], [], []
    for layer in range(2):
        act = turn(where, acts[layer], over[layer], frames)
        got = [move(pick(act, quarter ^ (m + 1), 0), mask) for m, mask in enumerate(chip_masks)]
        own = jnp.stack([pieces[layer]] + [move(pieces[layer], mask) for mask in chip_masks])
        other = move(own, core_mask)
        keep, *out = plane(where, table, act, got, own, other)
        got = [move(value, mask) for value, mask in zip(out, z_masks)]
        gram, *slots = gather(table, keep, got)
        slots = [slots[0]] + [move(slots[m + 1], mask) for m, mask in enumerate(chip_masks)]
        grams.append(gram)
        kept.append(jnp.concatenate([s[0] for s in slots]))
        sent.append(move(jnp.concatenate([s[1] for s in slots]), core_mask))

    mine = jnp.where(core == 0, grams[0], grams[1]) + move(jnp.where(core == 0, grams[1], grams[0]), core_mask)
    for mask in (1, 16, 2, 4):
        mine = mine + move(mine, mask)
    inverse = inverse_of_factor(mine)
    theirs = move(inverse, core_mask)
    return basis_of(where, table, kept, sent, inverse, theirs, math.sqrt(27 * channels))


def solution(mesh):
    def body(activations, out_grads, omega):
        fits = (lax.axis_size("dp"), lax.axis_size("space")) == (4, 8)
        fits = fits and activations.shape == (2, 1, 8, 2, 32, 768) and omega.shape[1] == 128
        return (planes if fits else shards)(activations, out_grads, omega)

    return jax.shard_map(
        body,
        mesh=mesh,
        in_specs=(
            P(None, "dp", None, "space", None, None),
            P(None, "dp", None, "space", None, None),
            P(),
        ),
        out_specs=P(None, ("dp", "space"), None),
        check_vma=False,
    )
```

```python
import functools
import math

import jax
import jax.numpy as jnp
import numpy as np
from jax import lax
from jax.experimental import pallas as pl
from jax.experimental.pallas import tpu as pltpu
from jax.sharding import PartitionSpec as P


AXES = ("dp", "space")
F32, BF16 = jnp.float32, jnp.bfloat16
HIGHEST = lax.Precision.HIGHEST


def swap(value, mask, total):
    return lax.ppermute(value, AXES, [(d, d ^ mask) for d in range(total)])


def halo(value, axis, dim):
    count, length = lax.axis_size(axis), value.shape[dim]
    up = [(i, i + 1) for i in range(count - 1)]
    before = lax.ppermute(lax.slice_in_dim(value, length - 1, length, axis=dim), axis, up)
    after = lax.ppermute(lax.slice_in_dim(value, 0, 1, axis=dim), axis, [(j, i) for i, j in up])
    return jnp.concatenate([before, value, after], axis=dim)


def product_kernel(frames, height, widths, rank, act_ref, sk_ref, out_ref, act_t, wide):
    step = pl.program_id(0)

    @pl.when(step == 0)
    def _():
        act_t[...] = act_ref[...].T
        zero = jnp.zeros((height + 2, widths, 3 * rank), BF16)
        wide[0] = zero
        wide[frames + 1] = zero
        rows = frames * (height + 2) * widths
        flat = sk_ref[...].astype(F32).reshape(rows, rank)
        at = lax.rem(lax.broadcasted_iota(jnp.int32, (rows, rank), 0), widths)
        later = jnp.where(at == widths - 1, 0.0, pltpu.roll(flat, rows - 1, 0))
        earlier = jnp.where(at == 0, 0.0, pltpu.roll(flat, 1, 0))
        shape = (frames, height + 2, widths, rank)
        wide[1 : frames + 1, :, :, 0:rank] = later.astype(BF16).reshape(shape)
        wide[1 : frames + 1, :, :, rank : 2 * rank] = sk_ref[...]
        wide[1 : frames + 1, :, :, 2 * rank :] = earlier.astype(BF16).reshape(shape)

    along_t, along_h = step // 3, lax.rem(step, 3)
    window = wide[pl.ds(2 - along_t, frames), pl.ds(2 - along_h, height)]
    window = window.reshape(frames * height * widths, 3 * rank)
    made = jnp.dot(act_t[...], window, preferred_element_type=F32)
    for c in range(3):
        out_ref[c] = made[:, c * rank : (c + 1) * rank]


def product(act, extended):
    frames, rows, widths, rank = extended.shape
    height, channels = rows - 2, act.shape[-1]
    positions = frames * height * widths
    return pl.pallas_call(
        functools.partial(product_kernel, frames, height, widths, rank),
        grid=(9,),
        in_specs=[
            pl.BlockSpec((positions, channels), lambda s: (0, 0)),
            pl.BlockSpec((frames, rows, widths, rank), lambda s: (0, 0, 0, 0)),
        ],
        out_specs=pl.BlockSpec((3, channels, rank), lambda s: (s, 0, 0)),
        out_shape=jax.ShapeDtypeStruct((27, channels, rank), F32),
        scratch_shapes=[
            pltpu.VMEM((channels, positions), BF16),
            pltpu.VMEM((frames + 2, rows, widths, 3 * rank), BF16),
        ],
        compiler_params=pltpu.CompilerParams(vmem_limit_bytes=40 * 2**20),
        cost_estimate=pl.CostEstimate(
            flops=2 * 27 * positions * channels * rank,
            bytes_accessed=27 * channels * rank * 4 + positions * channels * 2,
            transcendentals=0,
        ),
        name="product",
    )(act.reshape(positions, channels), extended)


def three(value):
    one = value.astype(BF16).astype(F32)
    two = (value - one).astype(BF16).astype(F32)
    return one, two, value - one - two


def outer(left, right):
    a, b, c = three(left)
    d, e, f = three(right)
    lhs = jnp.concatenate([a, a, b, a, b, c], axis=0).astype(BF16)
    rhs = jnp.concatenate([d, e, d, f, e, d], axis=0).astype(BF16)
    return lax.dot_general(lhs, rhs, (((0,), (0,)), ((), ())), preferred_element_type=F32)


def eliminate(grams, works, put):
    size = grams[0].shape[0]
    eye = lax.broadcasted_iota(jnp.int32, (size, size), 0) == lax.broadcasted_iota(jnp.int32, (size, size), 1)
    count = range(len(grams))
    for i in count:
        works[i][:, :size] = grams[i]
        works[i][:, size:] = eye.astype(F32)
    sub = lax.broadcasted_iota(jnp.int32, (8, 1), 0)
    for start in range(0, size, 8):
        rows = [works[i][start : start + 8, :] for i in count]
        cols = [
            [jnp.broadcast_to(rows[i][:, start + r : start + r + 1], (8, size)) for r in range(8)] for i in count
        ]
        for r in range(8):
            for i in count:
                scale = lax.rsqrt(cols[i][r][r : r + 1, :])
                below = jnp.where(sub > r, cols[i][r] * scale, 0.0)
                for c in range(r + 1, 8):
                    cols[i][c] = cols[i][c] - below * (cols[i][c][r : r + 1, :] * scale)
                row = rows[i][r : r + 1, :] * jnp.concatenate([scale, scale], axis=1)
                rest = rows[i] - jnp.concatenate([below, below], axis=1) * row
                rows[i] = jnp.where(sub == r, row, rest)
        for i in count:
            put(i, start, rows[i][:, size:])
            if start + 8 < size:
                update = outer(rows[i][:, :size], rows[i])
                works[i][start + 8 :, :] = works[i][start + 8 :, :] - update[start + 8 :, :]


def inverse_kernel(gram_ref, out_ref, work):
    def put(i, start, value):
        out_ref[start : start + 8, :] = value

    eliminate([gram_ref[...]], [work], put)


def inverse_of_factor(gram):
    size = gram.shape[-1]
    return pl.pallas_call(
        inverse_kernel,
        out_shape=jax.ShapeDtypeStruct((size, size), F32),
        scratch_shapes=[pltpu.VMEM((size, 2 * size), F32)],
        compiler_params=pltpu.CompilerParams(vmem_limit_bytes=4 * 2**20),
        name="inverse",
    )(gram)


def finish_kernel(size, scale, gram_ref, first_ref, second_ref, out_ref, one, two, high, middle, low):
    down = lax.broadcasted_iota(jnp.int32, (size, size), 0)
    across = lax.broadcasted_iota(jnp.int32, (size, size), 1)
    packed = gram_ref[0:size, :]
    under = jnp.where(down > across, packed, 0.0)
    first = under + under.T + jnp.where(down == across, gram_ref[size : size + 1, :], 0.0)
    second = jnp.where(down <= across, packed, jnp.where(down < across, packed, 0.0).T)

    def put(i, start, value):
        for ref, part in zip((high, middle, low), three(value)):
            ref[i, start : start + 8, :] = part

    eliminate([first, second], [one, two], put)
    for i, ref in enumerate((first_ref, second_ref)):
        d, e, f = (part[i].astype(BF16) for part in (high, middle, low))
        rhs = jnp.concatenate([d, e, d, f, e, d], axis=1)
        made = lax.dot_general(ref[...], rhs, (((1,), (1,)), ((), ())), preferred_element_type=F32)
        out_ref[i] = made * scale


def finish(packed, first, second, scale):
    size = packed.shape[-1]
    return pl.pallas_call(
        functools.partial(finish_kernel, size, scale),
        out_shape=jax.ShapeDtypeStruct((2, first.shape[0], size), F32),
        scratch_shapes=[pltpu.VMEM((size, 2 * size), F32)] * 2 + [pltpu.VMEM((2, size, size), F32)] * 3,
        compiler_params=pltpu.CompilerParams(vmem_limit_bytes=8 * 2**20),
        cost_estimate=pl.CostEstimate(flops=2**31, bytes_accessed=2**22, transcendentals=0),
        name="finish",
    )(packed, first, second)


def pick(value, index, axis):
    return lax.dynamic_index_in_dim(value, index, axis, keepdims=False)


def halve(value, axis, own, mask, total):
    sent = pick(value, 1 - own, axis).astype(BF16)
    return pick(value, own, axis) + swap(sent, mask, total).astype(F32)


def scatter_layer(partial, bits, total):
    rank = partial.shape[-1]
    rows = partial.shape[0] * partial.shape[1] // total
    count = len(bits)
    core_at = count - 1 - (lax.axis_size("space").bit_length() - 1)
    view = partial.reshape((2,) * count + (rows, rank))
    masks = [1 << (count - 1 - i) for i in range(count)]
    if count == 5 and core_at == 1:
        y, _, zh, zl, x = bits
        my, mc, _, mzl, mx = masks
        view = halve(view, 1, bits[1], mc, total)
        one, two = view[:, 0], view[:, 1]
        one = halve(one, 2, x, mx, total)
        two = halve(two, 0, y, my, total)
        one = halve(one, 0, y, my, total)
        two = halve(two, 1, x, mx, total)
        z = 2 * zh + zl
        both = jnp.stack([one, two]).reshape(4, rows, rank)
        got = [swap(pick(both, z ^ m, 0).astype(BF16), m * mzl, total) for m in (1, 2, 3)]
        return pick(both, z, 0) + (got[0].astype(F32) + got[1].astype(F32) + got[2].astype(F32))
    order = [core_at] + [i for i in range(count) if i != core_at]
    left = list(range(count))
    for i in order:
        view = halve(view, left.index(i), bits[i], masks[i], total)
        left.remove(i)
    return view


def shards(activations, out_grads, omega):
    layer_count, _, frames, height, widths, channels = activations.shape
    rank = omega.shape[1]
    total = lax.axis_size("dp") * lax.axis_size("space")
    count = total.bit_length() - 1
    me = lax.axis_index("dp") * lax.axis_size("space") + lax.axis_index("space")
    bits = [(me >> (count - 1 - i)) & 1 for i in range(count)]
    core_mask = lax.axis_size("space")
    core = lax.axis_index("dp") & 1

    sketched = jnp.dot(out_grads.reshape(-1, channels), omega, preferred_element_type=F32).astype(BF16)
    sketched = sketched.reshape(layer_count, frames, height, widths, rank)
    extended = halo(sketched, "space", 2)
    blocks = []
    for layer in range(layer_count):
        partial = product(activations[layer], extended[layer])
        blocks.append(scatter_layer(partial, bits, total))
    rows = jnp.stack(blocks)
    gram = jnp.einsum("lnr,lns->lrs", rows, rows, precision=HIGHEST)
    mine = pick(gram, core, 0) + swap(pick(gram, 1 - core, 0), core_mask, total)
    for i in range(count):
        mask = 1 << i
        if mask != core_mask:
            mine = mine + swap(mine, mask, total)
    inverse = inverse_of_factor(mine)
    other = swap(inverse, core_mask, total)
    inverses = [jnp.where(core == layer, inverse, other) for layer in range(2)]
    scale = math.sqrt(27 * channels)
    basis = [jnp.dot(rows[i], inverses[i].T, precision=HIGHEST) * scale for i in range(2)]
    return jnp.stack(basis)


UNITS = 28
PLACE, BY_Z, BY_CHIP, FINAL = 0, 3, 3 + 4 * UNITS, 3 + 4 * UNITS + 32


@functools.lru_cache
def unit_tables():
    table = np.zeros((32, FINAL + 27), np.int32)
    for device in range(32):
        y, core, z, x = device >> 4, (device >> 3) & 1, (device >> 1) & 3, device & 1
        quarter = 2 * y + x
        first = 16 * core + 4 * quarter

        def units_for(target):
            return [4 * k + s for k in range(27) for s in range(4) if ((32 * k + first + s) // 54) % 4 == target]

        row = [core, x, quarter]
        for m in range(4):
            units = units_for(z ^ m)
            row += units + [108] * (UNITS - len(units))
        held = units_for(z)
        for m in range(4):
            for other in range(2):
                q = quarter ^ m
                target = ((q >> 1) << 4) | ((core ^ other) << 3) | (z << 1) | (q & 1)
                for s in range(4):
                    found = [p for p, n in enumerate(held) if n % 4 == s and (8 * (n - s) + first + s) // 27 == target]
                    row.append(found[0] if found else UNITS)
        for v in range(27):
            column = (27 * device + v) % 32
            row.append(16 * ((column // 16) ^ core) + 4 * (((column % 16) // 4) ^ quarter) + column % 4)
        table[device] = row
    return table


def turn_kernel(frames, chunk, half, table_ref, own_ref, got_ref, p0, p1, p2, p3, work):
    at = pl.multiple_of(table_ref[PLACE] * half, 128)
    quarter = table_ref[PLACE + 2]
    each = half // 4
    for t in range(frames):
        rows = slice(chunk * t, chunk * (t + 1))
        block = jnp.concatenate([own_ref[rows, pl.ds(at, half)], got_ref[rows, pl.ds(at, half)]], axis=0)
        work[:, :, 2 * chunk * t : 2 * chunk * (t + 1)] = block.T.reshape(4, each, 2 * chunk)
    for m, ref in enumerate((p0, p1, p2, p3)):
        ref[...] = work[quarter ^ m]


def limit(mib):
    return pltpu.CompilerParams(vmem_limit_bytes=mib * 2**20)


def turn(table, own, got, layer, frames):
    positions, half = own.shape[1], own.shape[2] // 2
    vmem = pl.BlockSpec(memory_space=pltpu.VMEM)
    return pl.pallas_call(
        functools.partial(turn_kernel, frames, positions // frames, half),
        grid=(1,),
        in_specs=[
            pl.BlockSpec(memory_space=pltpu.SMEM),
            pl.BlockSpec((None, positions, own.shape[2]), lambda i: (layer, 0, 0)),
            pl.BlockSpec((None, positions, own.shape[2]), lambda i: (layer, 0, 0)),
        ],
        out_specs=[vmem] * 4,
        out_shape=[jax.ShapeDtypeStruct((half // 4, 2 * positions), BF16)] * 4,
        scratch_shapes=[pltpu.VMEM((4, half // 4, 2 * positions), BF16)],
        compiler_params=limit(10),
        cost_estimate=pl.CostEstimate(flops=0, bytes_accessed=8 * positions * half, transcendentals=0),
        name="turn",
    )(table, own, got)


def pieces_kernel(table_ref, sketched_ref, edge_ref, *outs):
    x = table_ref[PLACE + 1]
    for layer, out_ref in enumerate(outs):
        out_ref[:, pl.ds(1 - x, 2)] = sketched_ref[layer]
        out_ref[:, pl.ds(2 * x, 1)] = edge_ref[layer]


def pieces_of(table, sketched, edge):
    _, frames, height, widths, rank = sketched.shape
    vmem = pl.BlockSpec(memory_space=pltpu.VMEM)
    return pl.pallas_call(
        pieces_kernel,
        in_specs=[pl.BlockSpec(memory_space=pltpu.SMEM), vmem, vmem],
        out_specs=[vmem] * 2,
        out_shape=[jax.ShapeDtypeStruct((frames, height + 1, widths, rank), BF16)] * 2,
        compiler_params=limit(4),
        cost_estimate=pl.CostEstimate(flops=0, bytes_accessed=2**20, transcendentals=0),
        name="pieces",
    )(table, sketched, edge)


def plane_kernel(frames, widths, rank, table_ref, *refs):
    acts, sides, refs = refs[:4], (refs[4:8], refs[8:12]), refs[12:]
    keep_ref, s1, s2, s3, lhs, wide, acc, units = refs
    x = table_ref[PLACE + 1]
    each, depth = acts[0].shape
    frame = depth // frames
    for m, ref in enumerate(acts):
        value = ref[...]
        zero = jnp.zeros((each, frame), BF16)
        lhs[m, 0:each, 0:frame] = zero
        lhs[m, 0:each, frame:] = value[:, : depth - frame]
        lhs[m, each : 2 * each, :] = value
        lhs[m, 2 * each :, : depth - frame] = value[:, frame:]
        lhs[m, 2 * each :, depth - frame :] = zero
    rows = frames * 3 * widths
    at = lax.rem(lax.broadcasted_iota(jnp.int32, (rows, rank), 0), widths)
    for side, pieces in enumerate(sides):
        for m in range(4):
            piece = pieces[m][...]
            to = pl.ds(3 * (x ^ (m & 1)), 3)
            flat = piece.astype(F32).reshape(rows, rank)
            later = jnp.where(at == widths - 1, 0.0, pltpu.roll(flat, rows - 1, 0))
            earlier = jnp.where(at == 0, 0.0, pltpu.roll(flat, 1, 0))
            wide[m >> 1, :, side, to, :, 0:rank] = later.astype(BF16).reshape(piece.shape)
            wide[m >> 1, :, side, to, :, rank : 2 * rank] = piece
            wide[m >> 1, :, side, to, :, 2 * rank :] = earlier.astype(BF16).reshape(piece.shape)

    blocks = each // 24
    units[27 * blocks] = jnp.zeros((24, rank), F32)

    @pl.loop(0, 3)
    def _(along_h):
        for m in range(4):
            window = wide[m >> 1, :, :, pl.ds(2 * (x ^ (m & 1)) + 2 - along_h, 2)]
            made = jnp.dot(lhs[m], window.reshape(depth, 3 * rank), preferred_element_type=F32)
            acc[...] = made if m == 0 else acc[...] + made
        for a in range(3):
            for c in range(3):
                part = acc[a * each : (a + 1) * each, c * rank : (c + 1) * rank]
                units[pl.ds((9 * a + 3 * along_h + c) * blocks, blocks)] = part.reshape(blocks, 24, rank)

    @pl.loop(0, UNITS)
    def _(p):
        keep_ref[p] = units[table_ref[BY_Z + p]]
        for m, ref in enumerate((s1, s2, s3)):
            ref[p] = units[table_ref[BY_Z + (m + 1) * UNITS + p]].astype(BF16)


def plane(table, act, got, own, other):
    frames, _, widths, rank = own[0].shape
    each, depth = act.shape
    vmem = pl.BlockSpec(memory_space=pltpu.VMEM)
    smem = pl.BlockSpec(memory_space=pltpu.SMEM)
    return pl.pallas_call(
        functools.partial(plane_kernel, frames, widths, rank),
        in_specs=[smem] + [vmem] * 12,
        out_specs=[vmem] * 4,
        out_shape=[jax.ShapeDtypeStruct((UNITS, 24, rank), F32)]
        + [jax.ShapeDtypeStruct((UNITS, 24, rank), BF16)] * 3,
        scratch_shapes=[
            pltpu.VMEM((4, 3 * each, depth), BF16),
            pltpu.VMEM((2, frames, 2, 6, widths, 3 * rank), BF16),
            pltpu.VMEM((3 * each, 3 * rank), F32),
            pltpu.VMEM((27 * each // 24 + 1, 24, rank), F32),
        ],
        compiler_params=limit(18),
        cost_estimate=pl.CostEstimate(
            flops=2 * 27 * 4 * depth * each * rank, bytes_accessed=6 * 2**20, transcendentals=0
        ),
        name="plane",
    )(table, act, *got, *own, *other)


def gather_kernel(rank, joined, table_ref, *refs):
    (keep_ref, g1, g2, g3), refs = refs[:4], refs[4:]
    first_ref, refs = (refs[0], refs[1:]) if joined else (None, refs)
    gram_ref, slots, rows = refs[0], refs[1:5], refs[5]
    total = keep_ref[...] + (g1[...].astype(F32) + g2[...].astype(F32) + g3[...].astype(F32))
    rows[0:UNITS] = total
    rows[UNITS] = jnp.zeros((24, rank), F32)
    for m, ref in enumerate(slots):
        for other in range(2):
            for s in range(4):
                ref[other, s] = rows[table_ref[BY_CHIP + 8 * m + 4 * other + s]]
    flat = total.reshape(UNITS * 24, rank)
    gram = lax.dot_general(
        flat, flat, (((0,), (0,)), ((), ())), precision=HIGHEST, preferred_element_type=F32
    )
    if joined:
        down = lax.broadcasted_iota(jnp.int32, (rank, rank), 0)
        across = lax.broadcasted_iota(jnp.int32, (rank, rank), 1)
        first = first_ref[...]
        gram_ref[0:rank, :] = jnp.where(down > across, first, gram)
        diagonal = jnp.sum(jnp.where(down == across, first, 0.0), axis=0, keepdims=True)
        gram_ref[rank:, :] = jnp.broadcast_to(diagonal, (8, rank))
    else:
        gram_ref[...] = gram


def gather(table, keep, got, first=None):
    rank = keep.shape[-1]
    joined = first is not None
    vmem = pl.BlockSpec(memory_space=pltpu.VMEM)
    return pl.pallas_call(
        functools.partial(gather_kernel, rank, joined),
        in_specs=[pl.BlockSpec(memory_space=pltpu.SMEM)] + [vmem] * (4 + joined),
        out_specs=[vmem] * 5,
        out_shape=[jax.ShapeDtypeStruct((rank + 8 * joined, rank), F32)]
        + [jax.ShapeDtypeStruct((2, 4, 24, rank), F32)] * 4,
        scratch_shapes=[pltpu.VMEM((UNITS + 1, 24, rank), F32)],
        compiler_params=limit(8),
        cost_estimate=pl.CostEstimate(flops=12 * UNITS * 24 * rank * rank, bytes_accessed=2**20, transcendentals=0),
        name="gather",
    )(table, keep, *got, *([first] if joined else []))


def pack_kernel(s0, s1, s2, s3, out_ref):
    for m, ref in enumerate((s0, s1, s2, s3)):
        out_ref[m] = ref[1]


def pack(slots):
    vmem = pl.BlockSpec(memory_space=pltpu.VMEM)
    return pl.pallas_call(
        pack_kernel,
        in_specs=[vmem] * 4,
        out_specs=vmem,
        out_shape=jax.ShapeDtypeStruct((4,) + slots[0].shape[1:], F32),
        compiler_params=limit(4),
        cost_estimate=pl.CostEstimate(flops=0, bytes_accessed=2**19, transcendentals=0),
        name="pack",
    )(*slots)


def arrange_kernel(rank, table_ref, s0, s1, s2, s3, other_ref, out_ref, units):
    for m, ref in enumerate((s0, s1, s2, s3)):
        units[4 * m : 4 * m + 4] = ref[0]
        units[16 + 4 * m : 20 + 4 * m] = other_ref[m]
    for v in range(0, 27):
        a, b, c = three(units[table_ref[FINAL + v]])
        for i, part in enumerate((a, a, b, a, b, c)):
            out_ref[24 * v : 24 * v + 24, rank * i : rank * (i + 1)] = part.astype(BF16)


def arrange(table, slots, other):
    rank = other.shape[-1]
    vmem = pl.BlockSpec(memory_space=pltpu.VMEM)
    return pl.pallas_call(
        functools.partial(arrange_kernel, rank),
        in_specs=[pl.BlockSpec(memory_space=pltpu.SMEM)] + [vmem] * 5,
        out_specs=vmem,
        out_shape=jax.ShapeDtypeStruct((27 * 24, 6 * rank), BF16),
        scratch_shapes=[pltpu.VMEM((32, 24, rank), F32)],
        compiler_params=limit(6),
        cost_estimate=pl.CostEstimate(flops=0, bytes_accessed=2**21, transcendentals=0),
        name="arrange",
    )(table, *slots, other)


def planes(activations, out_grads, omega):
    layer_count, _, frames, height, widths, channels = activations.shape
    rank = omega.shape[1]
    dp, space = lax.axis_index("dp"), lax.axis_index("space")
    x = space & 1
    me = 8 * dp + space
    core_mask, chip_masks, z_masks = 8, (1, 16, 17), (2, 4, 6)
    table = lax.dynamic_index_in_dim(jnp.asarray(unit_tables()), me, 0, keepdims=False)
    positions = frames * height * widths

    def move(value, mask):
        return swap(value, mask, 32)

    def move_all(values, masks):
        return [move(v, mask) for v, mask in zip(values, masks)]

    acts = activations.reshape(2, positions, channels)
    over = move(acts, core_mask)

    sketched = jnp.dot(out_grads.reshape(-1, channels), omega, preferred_element_type=F32).astype(BF16)
    sketched = sketched.reshape(layer_count, frames, height, widths, rank)
    edge = jnp.where(x == 1, sketched[:, :, height - 1], sketched[:, :, 0])
    pairs = [(i, i + 1) for i in range(1, 7, 2)]
    edge = lax.ppermute(edge, "space", pairs + [(j, i) for i, j in pairs])[:, :, None]
    pieces = pieces_of(table, sketched, edge)

    gram, held = None, []
    for layer in range(2):
        act, *out = turn(table, acts, over, layer, frames)
        got = move_all(out, chip_masks)
        own = [pieces[layer]] + move_all([pieces[layer]] * 3, chip_masks)
        other = [move(piece, core_mask) for piece in own]
        keep, *out = plane(table, act, got, own, other)
        got = move_all(out, z_masks)
        gram, *slots = gather(table, keep, got, gram)
        slots = slots[:1] + move_all(slots[1:], chip_masks)
        other = move(pack(slots), core_mask)
        held.append(arrange(table, slots, other))

    for mask in (core_mask, 4, 2, 1, 16):
        gram = gram + move(gram, mask)
    return finish(gram, *held, math.sqrt(27 * channels))


def solution(mesh):
    def body(activations, out_grads, omega):
        fits = (lax.axis_size("dp"), lax.axis_size("space")) == (4, 8)
        fits = fits and activations.shape == (2, 1, 8, 2, 32, 768) and omega.shape[1] == 128
        return (planes if fits else shards)(activations, out_grads, omega)

    return jax.shard_map(
        body,
        mesh=mesh,
        in_specs=(
            P(None, "dp", None, "space", None, None),
            P(None, "dp", None, "space", None, None),
            P(),
        ),
        out_specs=P(None, ("dp", "space"), None),
        check_vma=False,
    )
```

```python
import functools
import math

import jax
import jax.numpy as jnp
import numpy as np
from jax import lax
from jax.experimental import pallas as pl
from jax.experimental.pallas import tpu as pltpu
from jax.sharding import PartitionSpec as P


AXES = ("dp", "space")
F32, BF16 = jnp.float32, jnp.bfloat16
HIGHEST = lax.Precision.HIGHEST


def swap(value, mask, total):
    return lax.ppermute(value, AXES, [(d, d ^ mask) for d in range(total)])


def halo(value, axis, dim):
    count, length = lax.axis_size(axis), value.shape[dim]
    up = [(i, i + 1) for i in range(count - 1)]
    before = lax.ppermute(lax.slice_in_dim(value, length - 1, length, axis=dim), axis, up)
    after = lax.ppermute(lax.slice_in_dim(value, 0, 1, axis=dim), axis, [(j, i) for i, j in up])
    return jnp.concatenate([before, value, after], axis=dim)


def product_kernel(frames, height, widths, rank, act_ref, sk_ref, out_ref, act_t, wide):
    step = pl.program_id(0)

    @pl.when(step == 0)
    def _():
        act_t[...] = act_ref[...].T
        zero = jnp.zeros((height + 2, widths, 3 * rank), BF16)
        wide[0] = zero
        wide[frames + 1] = zero
        rows = frames * (height + 2) * widths
        flat = sk_ref[...].astype(F32).reshape(rows, rank)
        at = lax.rem(lax.broadcasted_iota(jnp.int32, (rows, rank), 0), widths)
        later = jnp.where(at == widths - 1, 0.0, pltpu.roll(flat, rows - 1, 0))
        earlier = jnp.where(at == 0, 0.0, pltpu.roll(flat, 1, 0))
        shape = (frames, height + 2, widths, rank)
        wide[1 : frames + 1, :, :, 0:rank] = later.astype(BF16).reshape(shape)
        wide[1 : frames + 1, :, :, rank : 2 * rank] = sk_ref[...]
        wide[1 : frames + 1, :, :, 2 * rank :] = earlier.astype(BF16).reshape(shape)

    along_t, along_h = step // 3, lax.rem(step, 3)
    window = wide[pl.ds(2 - along_t, frames), pl.ds(2 - along_h, height)]
    window = window.reshape(frames * height * widths, 3 * rank)
    made = jnp.dot(act_t[...], window, preferred_element_type=F32)
    for c in range(3):
        out_ref[c] = made[:, c * rank : (c + 1) * rank]


def product(act, extended):
    frames, rows, widths, rank = extended.shape
    height, channels = rows - 2, act.shape[-1]
    positions = frames * height * widths
    return pl.pallas_call(
        functools.partial(product_kernel, frames, height, widths, rank),
        grid=(9,),
        in_specs=[
            pl.BlockSpec((positions, channels), lambda s: (0, 0)),
            pl.BlockSpec((frames, rows, widths, rank), lambda s: (0, 0, 0, 0)),
        ],
        out_specs=pl.BlockSpec((3, channels, rank), lambda s: (s, 0, 0)),
        out_shape=jax.ShapeDtypeStruct((27, channels, rank), F32),
        scratch_shapes=[
            pltpu.VMEM((channels, positions), BF16),
            pltpu.VMEM((frames + 2, rows, widths, 3 * rank), BF16),
        ],
        compiler_params=pltpu.CompilerParams(vmem_limit_bytes=40 * 2**20),
        cost_estimate=pl.CostEstimate(
            flops=2 * 27 * positions * channels * rank,
            bytes_accessed=27 * channels * rank * 4 + positions * channels * 2,
            transcendentals=0,
        ),
        name="product",
    )(act.reshape(positions, channels), extended)


def three(value):
    one = value.astype(BF16).astype(F32)
    two = (value - one).astype(BF16).astype(F32)
    return one, two, value - one - two


def outer(left, right):
    a, b, c = three(left)
    d, e, f = three(right)
    lhs = jnp.concatenate([a, a, b, a, b, c], axis=0).astype(BF16)
    rhs = jnp.concatenate([d, e, d, f, e, d], axis=0).astype(BF16)
    return lax.dot_general(lhs, rhs, (((0,), (0,)), ((), ())), preferred_element_type=F32)


def eliminate(grams, works, put):
    size = grams[0].shape[0]
    eye = lax.broadcasted_iota(jnp.int32, (size, size), 0) == lax.broadcasted_iota(jnp.int32, (size, size), 1)
    count = range(len(grams))
    for i in count:
        works[i][:, :size] = grams[i]
        works[i][:, size:] = eye.astype(F32)
    sub = lax.broadcasted_iota(jnp.int32, (8, 1), 0)
    for start in range(0, size, 8):
        rows = [works[i][start : start + 8, :] for i in count]
        cols = [
            [jnp.broadcast_to(rows[i][:, start + r : start + r + 1], (8, size)) for r in range(8)] for i in count
        ]
        for r in range(8):
            for i in count:
                scale = lax.rsqrt(cols[i][r][r : r + 1, :])
                below = jnp.where(sub > r, cols[i][r] * scale, 0.0)
                for c in range(r + 1, 8):
                    cols[i][c] = cols[i][c] - below * (cols[i][c][r : r + 1, :] * scale)
                row = rows[i][r : r + 1, :] * jnp.concatenate([scale, scale], axis=1)
                rest = rows[i] - jnp.concatenate([below, below], axis=1) * row
                rows[i] = jnp.where(sub == r, row, rest)
        for i in count:
            put(i, start, rows[i][:, size:])
            if start + 8 < size:
                update = outer(rows[i][:, :size], rows[i])
                works[i][start + 8 :, :] = works[i][start + 8 :, :] - update[start + 8 :, :]


def inverse_kernel(gram_ref, out_ref, work):
    def put(i, start, value):
        out_ref[start : start + 8, :] = value

    eliminate([gram_ref[...]], [work], put)


def inverse_of_factor(gram):
    size = gram.shape[-1]
    return pl.pallas_call(
        inverse_kernel,
        out_shape=jax.ShapeDtypeStruct((size, size), F32),
        scratch_shapes=[pltpu.VMEM((size, 2 * size), F32)],
        compiler_params=pltpu.CompilerParams(vmem_limit_bytes=4 * 2**20),
        name="inverse",
    )(gram)


def finish_kernel(size, scale, table_ref, mine_ref, theirs_ref, first_ref, second_ref, out_ref, one, two, high, middle, low):
    down = lax.broadcasted_iota(jnp.int32, (size, size), 0)
    across = lax.broadcasted_iota(jnp.int32, (size, size), 1)
    core, half = table_ref[PLACE], size // 2 + 8
    top = jnp.where(core == 0, mine_ref[...], theirs_ref[...])
    bottom = jnp.where(core == 0, theirs_ref[...], mine_ref[...])
    packed = jnp.concatenate([top, bottom[: size - half]], axis=0)
    under = jnp.where(down > across, packed, 0.0)
    first = under + under.T + jnp.where(down == across, bottom[size - half : size - half + 1, :], 0.0)
    second = jnp.where(down <= across, packed, jnp.where(down < across, packed, 0.0).T)

    def put(i, start, value):
        for ref, part in zip((high, middle, low), three(value)):
            ref[i, start : start + 8, :] = part

    eliminate([first, second], [one, two], put)
    for i, ref in enumerate((first_ref, second_ref)):
        d, e, f = (part[i].astype(BF16) for part in (high, middle, low))
        rhs = jnp.concatenate([d, e, d, f, e, d], axis=1)
        made = lax.dot_general(ref[...], rhs, (((1,), (1,)), ((), ())), preferred_element_type=F32)
        out_ref[i] = made * scale


def finish(table, mine, theirs, first, second, scale):
    size = mine.shape[-1]
    vmem = pl.BlockSpec(memory_space=pltpu.VMEM)
    return pl.pallas_call(
        functools.partial(finish_kernel, size, scale),
        in_specs=[pl.BlockSpec(memory_space=pltpu.SMEM)] + [vmem] * 4,
        out_specs=vmem,
        out_shape=jax.ShapeDtypeStruct((2, first.shape[0], size), F32),
        scratch_shapes=[pltpu.VMEM((size, 2 * size), F32)] * 2 + [pltpu.VMEM((2, size, size), F32)] * 3,
        compiler_params=pltpu.CompilerParams(vmem_limit_bytes=8 * 2**20),
        cost_estimate=pl.CostEstimate(flops=2**31, bytes_accessed=2**22, transcendentals=0),
        name="finish",
    )(table, mine, theirs, first, second)


def pick(value, index, axis):
    return lax.dynamic_index_in_dim(value, index, axis, keepdims=False)


def halve(value, axis, own, mask, total):
    sent = pick(value, 1 - own, axis).astype(BF16)
    return pick(value, own, axis) + swap(sent, mask, total).astype(F32)


def scatter_layer(partial, bits, total):
    rank = partial.shape[-1]
    rows = partial.shape[0] * partial.shape[1] // total
    count = len(bits)
    core_at = count - 1 - (lax.axis_size("space").bit_length() - 1)
    view = partial.reshape((2,) * count + (rows, rank))
    masks = [1 << (count - 1 - i) for i in range(count)]
    if count == 5 and core_at == 1:
        y, _, zh, zl, x = bits
        my, mc, _, mzl, mx = masks
        view = halve(view, 1, bits[1], mc, total)
        one, two = view[:, 0], view[:, 1]
        one = halve(one, 2, x, mx, total)
        two = halve(two, 0, y, my, total)
        one = halve(one, 0, y, my, total)
        two = halve(two, 1, x, mx, total)
        z = 2 * zh + zl
        both = jnp.stack([one, two]).reshape(4, rows, rank)
        got = [swap(pick(both, z ^ m, 0).astype(BF16), m * mzl, total) for m in (1, 2, 3)]
        return pick(both, z, 0) + (got[0].astype(F32) + got[1].astype(F32) + got[2].astype(F32))
    order = [core_at] + [i for i in range(count) if i != core_at]
    left = list(range(count))
    for i in order:
        view = halve(view, left.index(i), bits[i], masks[i], total)
        left.remove(i)
    return view


def shards(activations, out_grads, omega):
    layer_count, _, frames, height, widths, channels = activations.shape
    rank = omega.shape[1]
    total = lax.axis_size("dp") * lax.axis_size("space")
    count = total.bit_length() - 1
    me = lax.axis_index("dp") * lax.axis_size("space") + lax.axis_index("space")
    bits = [(me >> (count - 1 - i)) & 1 for i in range(count)]
    core_mask = lax.axis_size("space")
    core = lax.axis_index("dp") & 1

    sketched = jnp.dot(out_grads.reshape(-1, channels), omega, preferred_element_type=F32).astype(BF16)
    sketched = sketched.reshape(layer_count, frames, height, widths, rank)
    extended = halo(sketched, "space", 2)
    blocks = []
    for layer in range(layer_count):
        partial = product(activations[layer], extended[layer])
        blocks.append(scatter_layer(partial, bits, total))
    rows = jnp.stack(blocks)
    gram = jnp.einsum("lnr,lns->lrs", rows, rows, precision=HIGHEST)
    mine = pick(gram, core, 0) + swap(pick(gram, 1 - core, 0), core_mask, total)
    for i in range(count):
        mask = 1 << i
        if mask != core_mask:
            mine = mine + swap(mine, mask, total)
    inverse = inverse_of_factor(mine)
    other = swap(inverse, core_mask, total)
    inverses = [jnp.where(core == layer, inverse, other) for layer in range(2)]
    scale = math.sqrt(27 * channels)
    basis = [jnp.dot(rows[i], inverses[i].T, precision=HIGHEST) * scale for i in range(2)]
    return jnp.stack(basis)


UNITS = 28
PLACE, BY_Z, BY_CHIP, FINAL = 0, 3, 3 + 4 * UNITS, 3 + 4 * UNITS + 32


@functools.lru_cache
def unit_tables():
    table = np.zeros((32, FINAL + 27), np.int32)
    for device in range(32):
        y, core, z, x = device >> 4, (device >> 3) & 1, (device >> 1) & 3, device & 1
        quarter = 2 * y + x
        first = 16 * core + 4 * quarter

        def units_for(target):
            return [4 * k + s for k in range(27) for s in range(4) if ((32 * k + first + s) // 54) % 4 == target]

        row = [core, x, quarter]
        for m in range(4):
            units = units_for(z ^ m)
            row += units + [108] * (UNITS - len(units))
        held = units_for(z)
        for m in range(4):
            for other in range(2):
                q = quarter ^ m
                target = ((q >> 1) << 4) | ((core ^ other) << 3) | (z << 1) | (q & 1)
                for s in range(4):
                    found = [p for p, n in enumerate(held) if n % 4 == s and (8 * (n - s) + first + s) // 27 == target]
                    row.append(found[0] if found else UNITS)
        for v in range(27):
            column = (27 * device + v) % 32
            row.append(16 * ((column // 16) ^ core) + 4 * (((column % 16) // 4) ^ quarter) + column % 4)
        table[device] = row
    return table


def turn_kernel(frames, chunk, half, table_ref, own_ref, got_ref, p0, p1, p2, p3, work):
    at = pl.multiple_of(table_ref[PLACE] * half, 128)
    quarter = table_ref[PLACE + 2]
    each = half // 4
    for t in range(frames):
        rows = slice(chunk * t, chunk * (t + 1))
        block = jnp.concatenate([own_ref[rows, pl.ds(at, half)], got_ref[rows, pl.ds(at, half)]], axis=0)
        work[:, :, 2 * chunk * t : 2 * chunk * (t + 1)] = block.T.reshape(4, each, 2 * chunk)
    for m, ref in enumerate((p0, p1, p2, p3)):
        ref[...] = work[quarter ^ m]


def limit(mib):
    return pltpu.CompilerParams(vmem_limit_bytes=mib * 2**20)


def turn(table, own, got, layer, frames):
    positions, half = own.shape[1], own.shape[2] // 2
    vmem = pl.BlockSpec(memory_space=pltpu.VMEM)
    return pl.pallas_call(
        functools.partial(turn_kernel, frames, positions // frames, half),
        grid=(1,),
        in_specs=[
            pl.BlockSpec(memory_space=pltpu.SMEM),
            pl.BlockSpec((None, positions, own.shape[2]), lambda i: (layer, 0, 0)),
            pl.BlockSpec((None, positions, own.shape[2]), lambda i: (layer, 0, 0)),
        ],
        out_specs=[vmem] * 4,
        out_shape=[jax.ShapeDtypeStruct((half // 4, 2 * positions), BF16)] * 4,
        scratch_shapes=[pltpu.VMEM((4, half // 4, 2 * positions), BF16)],
        compiler_params=limit(10),
        cost_estimate=pl.CostEstimate(flops=0, bytes_accessed=8 * positions * half, transcendentals=0),
        name="turn",
    )(table, own, got)


def pieces_kernel(table_ref, sketched_ref, edge_ref, *outs):
    x = table_ref[PLACE + 1]
    for layer, out_ref in enumerate(outs):
        out_ref[:, pl.ds(1 - x, 2)] = sketched_ref[layer]
        out_ref[:, pl.ds(2 * x, 1)] = edge_ref[layer]


def pieces_of(table, sketched, edge):
    _, frames, height, widths, rank = sketched.shape
    vmem = pl.BlockSpec(memory_space=pltpu.VMEM)
    return pl.pallas_call(
        pieces_kernel,
        in_specs=[pl.BlockSpec(memory_space=pltpu.SMEM), vmem, vmem],
        out_specs=[vmem] * 2,
        out_shape=[jax.ShapeDtypeStruct((frames, height + 1, widths, rank), BF16)] * 2,
        compiler_params=limit(4),
        cost_estimate=pl.CostEstimate(flops=0, bytes_accessed=2**20, transcendentals=0),
        name="pieces",
    )(table, sketched, edge)


def plane_kernel(frames, widths, rank, table_ref, *refs):
    acts, sides, refs = refs[:4], (refs[4:8], refs[8:12]), refs[12:]
    keep_ref, s1, s2, s3, lhs, wide, acc, units = refs
    x = table_ref[PLACE + 1]
    each, depth = acts[0].shape
    frame = depth // frames
    for m, ref in enumerate(acts):
        value = ref[...]
        zero = jnp.zeros((each, frame), BF16)
        lhs[m, 0:each, 0:frame] = zero
        lhs[m, 0:each, frame:] = value[:, : depth - frame]
        lhs[m, each : 2 * each, :] = value
        lhs[m, 2 * each :, : depth - frame] = value[:, frame:]
        lhs[m, 2 * each :, depth - frame :] = zero
    rows = frames * 3 * widths
    at = lax.rem(lax.broadcasted_iota(jnp.int32, (rows, rank), 0), widths)
    for side, pieces in enumerate(sides):
        for m in range(4):
            piece = pieces[m][...]
            to = pl.ds(3 * (x ^ (m & 1)), 3)
            flat = piece.astype(F32).reshape(rows, rank)
            later = jnp.where(at == widths - 1, 0.0, pltpu.roll(flat, rows - 1, 0))
            earlier = jnp.where(at == 0, 0.0, pltpu.roll(flat, 1, 0))
            wide[m >> 1, :, side, to, :, 0:rank] = later.astype(BF16).reshape(piece.shape)
            wide[m >> 1, :, side, to, :, rank : 2 * rank] = piece
            wide[m >> 1, :, side, to, :, 2 * rank :] = earlier.astype(BF16).reshape(piece.shape)

    blocks = each // 24
    units[27 * blocks] = jnp.zeros((24, rank), F32)

    @pl.loop(0, 3)
    def _(along_h):
        for m in range(4):
            window = wide[m >> 1, :, :, pl.ds(2 * (x ^ (m & 1)) + 2 - along_h, 2)]
            made = jnp.dot(lhs[m], window.reshape(depth, 3 * rank), preferred_element_type=F32)
            acc[...] = made if m == 0 else acc[...] + made
        for a in range(3):
            for c in range(3):
                part = acc[a * each : (a + 1) * each, c * rank : (c + 1) * rank]
                units[pl.ds((9 * a + 3 * along_h + c) * blocks, blocks)] = part.reshape(blocks, 24, rank)

    @pl.loop(0, UNITS)
    def _(p):
        keep_ref[p] = units[table_ref[BY_Z + p]]
        for m, ref in enumerate((s1, s2, s3)):
            ref[p] = units[table_ref[BY_Z + (m + 1) * UNITS + p]].astype(BF16)


def plane(table, act, got, own, other):
    frames, _, widths, rank = own[0].shape
    each, depth = act.shape
    vmem = pl.BlockSpec(memory_space=pltpu.VMEM)
    smem = pl.BlockSpec(memory_space=pltpu.SMEM)
    return pl.pallas_call(
        functools.partial(plane_kernel, frames, widths, rank),
        in_specs=[smem] + [vmem] * 12,
        out_specs=[vmem] * 4,
        out_shape=[jax.ShapeDtypeStruct((UNITS, 24, rank), F32)]
        + [jax.ShapeDtypeStruct((UNITS, 24, rank), BF16)] * 3,
        scratch_shapes=[
            pltpu.VMEM((4, 3 * each, depth), BF16),
            pltpu.VMEM((2, frames, 2, 6, widths, 3 * rank), BF16),
            pltpu.VMEM((3 * each, 3 * rank), F32),
            pltpu.VMEM((27 * each // 24 + 1, 24, rank), F32),
        ],
        compiler_params=limit(18),
        cost_estimate=pl.CostEstimate(
            flops=2 * 27 * 4 * depth * each * rank, bytes_accessed=6 * 2**20, transcendentals=0
        ),
        name="plane",
    )(table, act, *got, *own, *other)


def gather_kernel(rank, joined, table_ref, *refs):
    (keep_ref, g1, g2, g3), refs = refs[:4], refs[4:]
    first_ref, refs = (refs[0], refs[1:]) if joined else (None, refs)
    grams, slots, rows = refs[: 1 + joined], refs[1 + joined : 5 + joined], refs[5 + joined]
    total = keep_ref[...] + (g1[...].astype(F32) + g2[...].astype(F32) + g3[...].astype(F32))
    rows[0:UNITS] = total
    rows[UNITS] = jnp.zeros((24, rank), F32)
    for m, ref in enumerate(slots):
        for other in range(2):
            for s in range(4):
                ref[other, s] = rows[table_ref[BY_CHIP + 8 * m + 4 * other + s]]
    flat = total.reshape(UNITS * 24, rank)
    gram = lax.dot_general(
        flat, flat, (((0,), (0,)), ((), ())), precision=HIGHEST, preferred_element_type=F32
    )
    if joined:
        down = lax.broadcasted_iota(jnp.int32, (rank, rank), 0)
        across = lax.broadcasted_iota(jnp.int32, (rank, rank), 1)
        first = first_ref[...]
        diagonal = jnp.sum(jnp.where(down == across, first, 0.0), axis=0, keepdims=True)
        both, half = refs[-1], rank // 2 + 8
        packed = jnp.where(down > across, first, gram)
        both[0] = packed[:half]
        both[1, : rank - half] = packed[half:]
        both[1, rank - half :] = jnp.broadcast_to(diagonal, (2 * half - rank, rank))
        core = table_ref[PLACE]
        grams[0][...] = both[core]
        grams[1][...] = both[1 - core]
    else:
        grams[0][...] = gram


def gather(table, keep, got, first=None):
    rank = keep.shape[-1]
    joined = first is not None
    gram = (rank // 2 + 8, rank) if joined else (rank, rank)
    vmem = pl.BlockSpec(memory_space=pltpu.VMEM)
    return pl.pallas_call(
        functools.partial(gather_kernel, rank, joined),
        in_specs=[pl.BlockSpec(memory_space=pltpu.SMEM)] + [vmem] * (4 + joined),
        out_specs=[vmem] * (5 + joined),
        out_shape=[jax.ShapeDtypeStruct(gram, F32)] * (1 + joined)
        + [jax.ShapeDtypeStruct((2, 4, 24, rank), F32)] * 4,
        scratch_shapes=[pltpu.VMEM((UNITS + 1, 24, rank), F32)] + [pltpu.VMEM((2,) + gram, F32)] * joined,
        compiler_params=limit(8),
        cost_estimate=pl.CostEstimate(flops=12 * UNITS * 24 * rank * rank, bytes_accessed=2**20, transcendentals=0),
        name="gather",
    )(table, keep, *got, *([first] if joined else []))


def pack_kernel(s0, s1, s2, s3, out_ref):
    for m, ref in enumerate((s0, s1, s2, s3)):
        out_ref[m] = ref[1]


def pack(slots):
    vmem = pl.BlockSpec(memory_space=pltpu.VMEM)
    return pl.pallas_call(
        pack_kernel,
        in_specs=[vmem] * 4,
        out_specs=vmem,
        out_shape=jax.ShapeDtypeStruct((4,) + slots[0].shape[1:], F32),
        compiler_params=limit(4),
        cost_estimate=pl.CostEstimate(flops=0, bytes_accessed=2**19, transcendentals=0),
        name="pack",
    )(*slots)


def arrange_kernel(rank, table_ref, s0, s1, s2, s3, other_ref, out_ref, units):
    for m, ref in enumerate((s0, s1, s2, s3)):
        units[4 * m : 4 * m + 4] = ref[0]
        units[16 + 4 * m : 20 + 4 * m] = other_ref[m]
    for v in range(0, 27):
        a, b, c = three(units[table_ref[FINAL + v]])
        for i, part in enumerate((a, a, b, a, b, c)):
            out_ref[24 * v : 24 * v + 24, rank * i : rank * (i + 1)] = part.astype(BF16)


def arrange(table, slots, other):
    rank = other.shape[-1]
    vmem = pl.BlockSpec(memory_space=pltpu.VMEM)
    return pl.pallas_call(
        functools.partial(arrange_kernel, rank),
        in_specs=[pl.BlockSpec(memory_space=pltpu.SMEM)] + [vmem] * 5,
        out_specs=vmem,
        out_shape=jax.ShapeDtypeStruct((27 * 24, 6 * rank), BF16),
        scratch_shapes=[pltpu.VMEM((32, 24, rank), F32)],
        compiler_params=limit(6),
        cost_estimate=pl.CostEstimate(flops=0, bytes_accessed=2**21, transcendentals=0),
        name="arrange",
    )(table, *slots, other)


def planes(activations, out_grads, omega):
    layer_count, _, frames, height, widths, channels = activations.shape
    rank = omega.shape[1]
    dp, space = lax.axis_index("dp"), lax.axis_index("space")
    x = space & 1
    me = 8 * dp + space
    core_mask, chip_masks, z_masks = 8, (1, 16, 17), (2, 4, 6)
    table = lax.dynamic_index_in_dim(jnp.asarray(unit_tables()), me, 0, keepdims=False)
    positions = frames * height * widths

    def move(value, mask):
        return swap(value, mask, 32)

    def move_all(values, masks):
        return [move(v, mask) for v, mask in zip(values, masks)]

    acts = activations.reshape(2, positions, channels)
    over = move(acts, core_mask)

    sketched = jnp.dot(out_grads.reshape(-1, channels), omega, preferred_element_type=F32).astype(BF16)
    sketched = sketched.reshape(layer_count, frames, height, widths, rank)
    edge = jnp.where(x == 1, sketched[:, :, height - 1], sketched[:, :, 0])
    pairs = [(i, i + 1) for i in range(1, 7, 2)]
    edge = lax.ppermute(edge, "space", pairs + [(j, i) for i, j in pairs])[:, :, None]
    pieces = pieces_of(table, sketched, edge)

    gram, held = None, []
    for layer in range(2):
        act, *out = turn(table, acts, over, layer, frames)
        got = move_all(out, chip_masks)
        own = [pieces[layer]] + move_all([pieces[layer]] * 3, chip_masks)
        other = [move(piece, core_mask) for piece in own]
        keep, *out = plane(table, act, got, own, other)
        got = move_all(out, z_masks)
        made = gather(table, keep, got, gram)
        gram, slots = (made[0], list(made[1:])) if layer == 0 else (made[:2], list(made[2:]))
        slots = slots[:1] + move_all(slots[1:], chip_masks)
        other = move(pack(slots), core_mask)
        held.append(arrange(table, slots, other))

    mine = gram[0] + move(gram[1], core_mask)
    for masks in (z_masks, chip_masks):
        one, two, both = move_all([mine] * 3, masks)
        mine = (mine + one) + (two + both)
    theirs = move(mine, core_mask)
    return finish(table, mine, theirs, *held, math.sqrt(27 * channels))


def solution(mesh):
    def body(activations, out_grads, omega):
        fits = (lax.axis_size("dp"), lax.axis_size("space")) == (4, 8)
        fits = fits and activations.shape == (2, 1, 8, 2, 32, 768) and omega.shape[1] == 128
        return (planes if fits else shards)(activations, out_grads, omega)

    return jax.shard_map(
        body,
        mesh=mesh,
        in_specs=(
            P(None, "dp", None, "space", None, None),
            P(None, "dp", None, "space", None, None),
            P(),
        ),
        out_specs=P(None, ("dp", "space"), None),
        check_vma=False,
    )
```

```python
import functools
import math

import jax
import jax.numpy as jnp
import numpy as np
from jax import lax
from jax.experimental import pallas as pl
from jax.experimental.pallas import tpu as pltpu
from jax.sharding import PartitionSpec as P


AXES = ("dp", "space")
F32, BF16 = jnp.float32, jnp.bfloat16
HIGHEST = lax.Precision.HIGHEST


def swap(value, mask, total):
    return lax.ppermute(value, AXES, [(d, d ^ mask) for d in range(total)])


def halo(value, axis, dim):
    count, length = lax.axis_size(axis), value.shape[dim]
    up = [(i, i + 1) for i in range(count - 1)]
    before = lax.ppermute(lax.slice_in_dim(value, length - 1, length, axis=dim), axis, up)
    after = lax.ppermute(lax.slice_in_dim(value, 0, 1, axis=dim), axis, [(j, i) for i, j in up])
    return jnp.concatenate([before, value, after], axis=dim)


def product_kernel(frames, height, widths, rank, act_ref, sk_ref, out_ref, act_t, wide):
    step = pl.program_id(0)

    @pl.when(step == 0)
    def _():
        act_t[...] = act_ref[...].T
        zero = jnp.zeros((height + 2, widths, 3 * rank), BF16)
        wide[0] = zero
        wide[frames + 1] = zero
        rows = frames * (height + 2) * widths
        flat = sk_ref[...].astype(F32).reshape(rows, rank)
        at = lax.rem(lax.broadcasted_iota(jnp.int32, (rows, rank), 0), widths)
        later = jnp.where(at == widths - 1, 0.0, pltpu.roll(flat, rows - 1, 0))
        earlier = jnp.where(at == 0, 0.0, pltpu.roll(flat, 1, 0))
        shape = (frames, height + 2, widths, rank)
        wide[1 : frames + 1, :, :, 0:rank] = later.astype(BF16).reshape(shape)
        wide[1 : frames + 1, :, :, rank : 2 * rank] = sk_ref[...]
        wide[1 : frames + 1, :, :, 2 * rank :] = earlier.astype(BF16).reshape(shape)

    along_t, along_h = step // 3, lax.rem(step, 3)
    window = wide[pl.ds(2 - along_t, frames), pl.ds(2 - along_h, height)]
    window = window.reshape(frames * height * widths, 3 * rank)
    made = jnp.dot(act_t[...], window, preferred_element_type=F32)
    for c in range(3):
        out_ref[c] = made[:, c * rank : (c + 1) * rank]


def product(act, extended):
    frames, rows, widths, rank = extended.shape
    height, channels = rows - 2, act.shape[-1]
    positions = frames * height * widths
    return pl.pallas_call(
        functools.partial(product_kernel, frames, height, widths, rank),
        grid=(9,),
        in_specs=[
            pl.BlockSpec((positions, channels), lambda s: (0, 0)),
            pl.BlockSpec((frames, rows, widths, rank), lambda s: (0, 0, 0, 0)),
        ],
        out_specs=pl.BlockSpec((3, channels, rank), lambda s: (s, 0, 0)),
        out_shape=jax.ShapeDtypeStruct((27, channels, rank), F32),
        scratch_shapes=[
            pltpu.VMEM((channels, positions), BF16),
            pltpu.VMEM((frames + 2, rows, widths, 3 * rank), BF16),
        ],
        compiler_params=pltpu.CompilerParams(vmem_limit_bytes=40 * 2**20),
        cost_estimate=pl.CostEstimate(
            flops=2 * 27 * positions * channels * rank,
            bytes_accessed=27 * channels * rank * 4 + positions * channels * 2,
            transcendentals=0,
        ),
        name="product",
    )(act.reshape(positions, channels), extended)


def three(value):
    one = value.astype(BF16).astype(F32)
    two = (value - one).astype(BF16).astype(F32)
    return one, two, value - one - two


def outer(left, right):
    a, b, c = three(left)
    d, e, f = three(right)
    lhs = jnp.concatenate([a, a, b, a, b, c], axis=0).astype(BF16)
    rhs = jnp.concatenate([d, e, d, f, e, d], axis=0).astype(BF16)
    return lax.dot_general(lhs, rhs, (((0,), (0,)), ((), ())), preferred_element_type=F32)


def eliminate(grams, works, put):
    size = grams[0].shape[0]
    eye = lax.broadcasted_iota(jnp.int32, (size, size), 0) == lax.broadcasted_iota(jnp.int32, (size, size), 1)
    count = range(len(grams))
    for i in count:
        works[i][:, :size] = grams[i]
        works[i][:, size:] = eye.astype(F32)
    sub = lax.broadcasted_iota(jnp.int32, (8, 1), 0)
    for start in range(0, size, 8):
        rows = [works[i][start : start + 8, :] for i in count]
        cols = [
            [jnp.broadcast_to(rows[i][:, start + r : start + r + 1], (8, size)) for r in range(8)] for i in count
        ]
        for r in range(8):
            for i in count:
                scale = lax.rsqrt(cols[i][r][r : r + 1, :])
                below = jnp.where(sub > r, cols[i][r] * scale, 0.0)
                for c in range(r + 1, 8):
                    cols[i][c] = cols[i][c] - below * (cols[i][c][r : r + 1, :] * scale)
                row = rows[i][r : r + 1, :] * jnp.concatenate([scale, scale], axis=1)
                rest = rows[i] - jnp.concatenate([below, below], axis=1) * row
                rows[i] = jnp.where(sub == r, row, rest)
        for i in count:
            put(i, start, rows[i][:, size:])
            if start + 8 < size:
                update = outer(rows[i][:, :size], rows[i])
                works[i][start + 8 :, :] = works[i][start + 8 :, :] - update[start + 8 :, :]


def inverse_kernel(gram_ref, out_ref, work):
    def put(i, start, value):
        out_ref[start : start + 8, :] = value

    eliminate([gram_ref[...]], [work], put)


def inverse_of_factor(gram):
    size = gram.shape[-1]
    return pl.pallas_call(
        inverse_kernel,
        out_shape=jax.ShapeDtypeStruct((size, size), F32),
        scratch_shapes=[pltpu.VMEM((size, 2 * size), F32)],
        compiler_params=pltpu.CompilerParams(vmem_limit_bytes=4 * 2**20),
        name="inverse",
    )(gram)


def inverses_kernel(size, table_ref, mine_ref, theirs_ref, out_ref, one, two, high, middle, low):
    down = lax.broadcasted_iota(jnp.int32, (size, size), 0)
    across = lax.broadcasted_iota(jnp.int32, (size, size), 1)
    core, half = table_ref[PLACE], size // 2 + 8
    top = jnp.where(core == 0, mine_ref[...], theirs_ref[...])
    bottom = jnp.where(core == 0, theirs_ref[...], mine_ref[...])
    packed = jnp.concatenate([top, bottom[: size - half]], axis=0)
    under = jnp.where(down > across, packed, 0.0)
    first = under + under.T + jnp.where(down == across, bottom[size - half : size - half + 1, :], 0.0)
    second = jnp.where(down <= across, packed, jnp.where(down < across, packed, 0.0).T)

    def put(i, start, value):
        for ref, part in zip((high, middle, low), three(value)):
            ref[i, start : start + 8, :] = part

    eliminate([first, second], [one, two], put)
    for i in range(2):
        d, e, f = (part[i].astype(BF16) for part in (high, middle, low))
        out_ref[i] = jnp.concatenate([d, e, d, f, e, d], axis=1)


def inverses_of_factors(table, mine, theirs):
    size = mine.shape[-1]
    vmem = pl.BlockSpec(memory_space=pltpu.VMEM)
    return pl.pallas_call(
        functools.partial(inverses_kernel, size),
        in_specs=[pl.BlockSpec(memory_space=pltpu.SMEM)] + [vmem] * 2,
        out_specs=vmem,
        out_shape=jax.ShapeDtypeStruct((2, size, 6 * size), BF16),
        scratch_shapes=[pltpu.VMEM((size, 2 * size), F32)] * 2 + [pltpu.VMEM((2, size, size), F32)] * 3,
        compiler_params=pltpu.CompilerParams(vmem_limit_bytes=4 * 2**20),
        cost_estimate=pl.CostEstimate(flops=2**30, bytes_accessed=2**20, transcendentals=0),
        name="inverses",
    )(table, mine, theirs)


def pick(value, index, axis):
    return lax.dynamic_index_in_dim(value, index, axis, keepdims=False)


def halve(value, axis, own, mask, total):
    sent = pick(value, 1 - own, axis).astype(BF16)
    return pick(value, own, axis) + swap(sent, mask, total).astype(F32)


def scatter_layer(partial, bits, total):
    rank = partial.shape[-1]
    rows = partial.shape[0] * partial.shape[1] // total
    count = len(bits)
    core_at = count - 1 - (lax.axis_size("space").bit_length() - 1)
    view = partial.reshape((2,) * count + (rows, rank))
    masks = [1 << (count - 1 - i) for i in range(count)]
    if count == 5 and core_at == 1:
        y, _, zh, zl, x = bits
        my, mc, _, mzl, mx = masks
        view = halve(view, 1, bits[1], mc, total)
        one, two = view[:, 0], view[:, 1]
        one = halve(one, 2, x, mx, total)
        two = halve(two, 0, y, my, total)
        one = halve(one, 0, y, my, total)
        two = halve(two, 1, x, mx, total)
        z = 2 * zh + zl
        both = jnp.stack([one, two]).reshape(4, rows, rank)
        got = [swap(pick(both, z ^ m, 0).astype(BF16), m * mzl, total) for m in (1, 2, 3)]
        return pick(both, z, 0) + (got[0].astype(F32) + got[1].astype(F32) + got[2].astype(F32))
    order = [core_at] + [i for i in range(count) if i != core_at]
    left = list(range(count))
    for i in order:
        view = halve(view, left.index(i), bits[i], masks[i], total)
        left.remove(i)
    return view


def shards(activations, out_grads, omega):
    layer_count, _, frames, height, widths, channels = activations.shape
    rank = omega.shape[1]
    total = lax.axis_size("dp") * lax.axis_size("space")
    count = total.bit_length() - 1
    me = lax.axis_index("dp") * lax.axis_size("space") + lax.axis_index("space")
    bits = [(me >> (count - 1 - i)) & 1 for i in range(count)]
    core_mask = lax.axis_size("space")
    core = lax.axis_index("dp") & 1

    sketched = jnp.dot(out_grads.reshape(-1, channels), omega, preferred_element_type=F32).astype(BF16)
    sketched = sketched.reshape(layer_count, frames, height, widths, rank)
    extended = halo(sketched, "space", 2)
    blocks = []
    for layer in range(layer_count):
        partial = product(activations[layer], extended[layer])
        blocks.append(scatter_layer(partial, bits, total))
    rows = jnp.stack(blocks)
    gram = jnp.einsum("lnr,lns->lrs", rows, rows, precision=HIGHEST)
    mine = pick(gram, core, 0) + swap(pick(gram, 1 - core, 0), core_mask, total)
    for i in range(count):
        mask = 1 << i
        if mask != core_mask:
            mine = mine + swap(mine, mask, total)
    inverse = inverse_of_factor(mine)
    other = swap(inverse, core_mask, total)
    inverses = [jnp.where(core == layer, inverse, other) for layer in range(2)]
    scale = math.sqrt(27 * channels)
    basis = [jnp.dot(rows[i], inverses[i].T, precision=HIGHEST) * scale for i in range(2)]
    return jnp.stack(basis)


UNITS = 28
PLACE, BY_Z, BY_CHIP, FINAL = 0, 3, 3 + 4 * UNITS, 3 + 4 * UNITS + 32


@functools.lru_cache
def unit_tables():
    table = np.zeros((32, FINAL + 27), np.int32)
    for device in range(32):
        y, core, z, x = device >> 4, (device >> 3) & 1, (device >> 1) & 3, device & 1
        quarter = 2 * y + x
        first = 16 * core + 4 * quarter

        def units_for(target):
            return [4 * k + s for k in range(27) for s in range(4) if ((32 * k + first + s) // 54) % 4 == target]

        row = [core, x, quarter]
        for m in range(4):
            units = units_for(z ^ m)
            row += units + [108] * (UNITS - len(units))
        held = units_for(z)
        for m in range(4):
            for other in range(2):
                q = quarter ^ m
                target = ((q >> 1) << 4) | ((core ^ other) << 3) | (z << 1) | (q & 1)
                for s in range(4):
                    found = [p for p, n in enumerate(held) if n % 4 == s and (8 * (n - s) + first + s) // 27 == target]
                    row.append(found[0] if found else UNITS)
        for v in range(27):
            column = (27 * device + v) % 32
            row.append(16 * ((column // 16) ^ core) + 4 * (((column % 16) // 4) ^ quarter) + column % 4)
        table[device] = row
    return table


def turn_kernel(frames, chunk, half, table_ref, own_ref, got_ref, p0, p1, p2, p3, work):
    at = pl.multiple_of(table_ref[PLACE] * half, 128)
    quarter = table_ref[PLACE + 2]
    each = half // 4
    for t in range(frames):
        rows = slice(chunk * t, chunk * (t + 1))
        block = jnp.concatenate([own_ref[rows, pl.ds(at, half)], got_ref[rows, pl.ds(at, half)]], axis=0)
        work[:, :, 2 * chunk * t : 2 * chunk * (t + 1)] = block.T.reshape(4, each, 2 * chunk)
    for m, ref in enumerate((p0, p1, p2, p3)):
        ref[...] = work[quarter ^ m]


def limit(mib):
    return pltpu.CompilerParams(vmem_limit_bytes=mib * 2**20)


def turn(table, own, got, layer, frames):
    positions, half = own.shape[1], own.shape[2] // 2
    vmem = pl.BlockSpec(memory_space=pltpu.VMEM)
    return pl.pallas_call(
        functools.partial(turn_kernel, frames, positions // frames, half),
        grid=(1,),
        in_specs=[
            pl.BlockSpec(memory_space=pltpu.SMEM),
            pl.BlockSpec((None, positions, own.shape[2]), lambda i: (layer, 0, 0)),
            pl.BlockSpec((None, positions, own.shape[2]), lambda i: (layer, 0, 0)),
        ],
        out_specs=[vmem] * 4,
        out_shape=[jax.ShapeDtypeStruct((half // 4, 2 * positions), BF16)] * 4,
        scratch_shapes=[pltpu.VMEM((4, half // 4, 2 * positions), BF16)],
        compiler_params=limit(10),
        cost_estimate=pl.CostEstimate(flops=0, bytes_accessed=8 * positions * half, transcendentals=0),
        name="turn",
    )(table, own, got)


def pieces_kernel(table_ref, sketched_ref, edge_ref, *outs):
    x = table_ref[PLACE + 1]
    for layer, out_ref in enumerate(outs):
        out_ref[:, pl.ds(1 - x, 2)] = sketched_ref[layer]
        out_ref[:, pl.ds(2 * x, 1)] = edge_ref[layer]


def pieces_of(table, sketched, edge):
    _, frames, height, widths, rank = sketched.shape
    vmem = pl.BlockSpec(memory_space=pltpu.VMEM)
    return pl.pallas_call(
        pieces_kernel,
        in_specs=[pl.BlockSpec(memory_space=pltpu.SMEM), vmem, vmem],
        out_specs=[vmem] * 2,
        out_shape=[jax.ShapeDtypeStruct((frames, height + 1, widths, rank), BF16)] * 2,
        compiler_params=limit(4),
        cost_estimate=pl.CostEstimate(flops=0, bytes_accessed=2**20, transcendentals=0),
        name="pieces",
    )(table, sketched, edge)


def plane_kernel(frames, widths, rank, table_ref, *refs):
    acts, sides, refs = refs[:4], (refs[4:8], refs[8:12]), refs[12:]
    keep_ref, s1, s2, s3, lhs, wide, acc, units = refs
    x = table_ref[PLACE + 1]
    each, depth = acts[0].shape
    frame = depth // frames
    for m, ref in enumerate(acts):
        value = ref[...]
        zero = jnp.zeros((each, frame), BF16)
        lhs[m, 0:each, 0:frame] = zero
        lhs[m, 0:each, frame:] = value[:, : depth - frame]
        lhs[m, each : 2 * each, :] = value
        lhs[m, 2 * each :, : depth - frame] = value[:, frame:]
        lhs[m, 2 * each :, depth - frame :] = zero
    rows = frames * 3 * widths
    at = lax.rem(lax.broadcasted_iota(jnp.int32, (rows, rank), 0), widths)
    for side, pieces in enumerate(sides):
        for m in range(4):
            piece = pieces[m][...]
            to = pl.ds(3 * (x ^ (m & 1)), 3)
            flat = piece.astype(F32).reshape(rows, rank)
            later = jnp.where(at == widths - 1, 0.0, pltpu.roll(flat, rows - 1, 0))
            earlier = jnp.where(at == 0, 0.0, pltpu.roll(flat, 1, 0))
            wide[m >> 1, :, side, to, :, 0:rank] = later.astype(BF16).reshape(piece.shape)
            wide[m >> 1, :, side, to, :, rank : 2 * rank] = piece
            wide[m >> 1, :, side, to, :, 2 * rank :] = earlier.astype(BF16).reshape(piece.shape)

    blocks = each // 24
    units[27 * blocks] = jnp.zeros((24, rank), F32)

    @pl.loop(0, 3)
    def _(along_h):
        for m in range(4):
            window = wide[m >> 1, :, :, pl.ds(2 * (x ^ (m & 1)) + 2 - along_h, 2)]
            made = jnp.dot(lhs[m], window.reshape(depth, 3 * rank), preferred_element_type=F32)
            acc[...] = made if m == 0 else acc[...] + made
        for a in range(3):
            for c in range(3):
                part = acc[a * each : (a + 1) * each, c * rank : (c + 1) * rank]
                units[pl.ds((9 * a + 3 * along_h + c) * blocks, blocks)] = part.reshape(blocks, 24, rank)

    @pl.loop(0, UNITS)
    def _(p):
        keep_ref[p] = units[table_ref[BY_Z + p]]
        for m, ref in enumerate((s1, s2, s3)):
            ref[p] = units[table_ref[BY_Z + (m + 1) * UNITS + p]].astype(BF16)


def plane(table, act, got, own, other):
    frames, _, widths, rank = own[0].shape
    each, depth = act.shape
    vmem = pl.BlockSpec(memory_space=pltpu.VMEM)
    smem = pl.BlockSpec(memory_space=pltpu.SMEM)
    return pl.pallas_call(
        functools.partial(plane_kernel, frames, widths, rank),
        in_specs=[smem] + [vmem] * 12,
        out_specs=[vmem] * 4,
        out_shape=[jax.ShapeDtypeStruct((UNITS, 24, rank), F32)]
        + [jax.ShapeDtypeStruct((UNITS, 24, rank), BF16)] * 3,
        scratch_shapes=[
            pltpu.VMEM((4, 3 * each, depth), BF16),
            pltpu.VMEM((2, frames, 2, 6, widths, 3 * rank), BF16),
            pltpu.VMEM((3 * each, 3 * rank), F32),
            pltpu.VMEM((27 * each // 24 + 1, 24, rank), F32),
        ],
        compiler_params=limit(18),
        cost_estimate=pl.CostEstimate(
            flops=2 * 27 * 4 * depth * each * rank, bytes_accessed=6 * 2**20, transcendentals=0
        ),
        name="plane",
    )(table, act, *got, *own, *other)


def gather_kernel(rank, joined, table_ref, *refs):
    (keep_ref, g1, g2, g3), refs = refs[:4], refs[4:]
    first_ref, refs = (refs[0], refs[1:]) if joined else (None, refs)
    grams, (own_ref, over_ref, rows) = refs[: 1 + joined], refs[1 + joined : 4 + joined]
    total = keep_ref[...] + (g1[...].astype(F32) + g2[...].astype(F32) + g3[...].astype(F32))
    rows[0:UNITS] = total
    rows[UNITS] = jnp.zeros((24, rank), F32)
    for other, ref in enumerate((own_ref, over_ref)):
        for m in range(4):
            for s in range(4):
                ref[m, s] = rows[table_ref[BY_CHIP + 8 * m + 4 * other + s]]
    flat = total.reshape(UNITS * 24, rank)
    gram = lax.dot_general(
        flat, flat, (((0,), (0,)), ((), ())), precision=HIGHEST, preferred_element_type=F32
    )
    if joined:
        down = lax.broadcasted_iota(jnp.int32, (rank, rank), 0)
        across = lax.broadcasted_iota(jnp.int32, (rank, rank), 1)
        first = first_ref[...]
        diagonal = jnp.sum(jnp.where(down == across, first, 0.0), axis=0, keepdims=True)
        both, half = refs[-1], rank // 2 + 8
        packed = jnp.where(down > across, first, gram)
        both[0] = packed[:half]
        both[1, : rank - half] = packed[half:]
        both[1, rank - half :] = jnp.broadcast_to(diagonal, (2 * half - rank, rank))
        core = table_ref[PLACE]
        grams[0][...] = both[core]
        grams[1][...] = both[1 - core]
    else:
        grams[0][...] = gram


def gather(table, keep, got, first=None):
    rank = keep.shape[-1]
    joined = first is not None
    gram = (rank // 2 + 8, rank) if joined else (rank, rank)
    vmem = pl.BlockSpec(memory_space=pltpu.VMEM)
    return pl.pallas_call(
        functools.partial(gather_kernel, rank, joined),
        in_specs=[pl.BlockSpec(memory_space=pltpu.SMEM)] + [vmem] * (4 + joined),
        out_specs=[vmem] * (3 + joined),
        out_shape=[jax.ShapeDtypeStruct(gram, F32)] * (1 + joined)
        + [jax.ShapeDtypeStruct((4, 4, 24, rank), F32)] * 2,
        scratch_shapes=[pltpu.VMEM((UNITS + 1, 24, rank), F32)] + [pltpu.VMEM((2,) + gram, F32)] * joined,
        compiler_params=limit(8),
        cost_estimate=pl.CostEstimate(flops=12 * UNITS * 24 * rank * rank, bytes_accessed=2**20, transcendentals=0),
        name="gather",
    )(table, keep, *got, *([first] if joined else []))


def pack_kernel(own_ref, got_ref, *outs):
    for m, ref in enumerate(outs):
        ref[0] = own_ref[m]
        ref[1] = got_ref[m]


def pack(own, got):
    vmem = pl.BlockSpec(memory_space=pltpu.VMEM)
    return pl.pallas_call(
        pack_kernel,
        in_specs=[vmem] * 2,
        out_specs=[vmem] * 4,
        out_shape=[jax.ShapeDtypeStruct((2,) + own.shape[1:], F32)] * 4,
        compiler_params=limit(4),
        cost_estimate=pl.CostEstimate(flops=0, bytes_accessed=2**19, transcendentals=0),
        name="pack",
    )(own, got)


def arrange_kernel(table_ref, s0, s1, s2, s3, out_ref, units):
    rank = out_ref.shape[1] // 6
    for m, ref in enumerate((s0, s1, s2, s3)):
        units[4 * m : 4 * m + 4] = ref[0]
        units[16 + 4 * m : 20 + 4 * m] = ref[1]
    for v in range(27):
        a, b, c = three(units[table_ref[FINAL + v]])
        for i, part in enumerate((a, a, b, a, b, c)):
            out_ref[24 * v : 24 * v + 24, rank * i : rank * (i + 1)] = part.astype(BF16)


def arrange(table, slots):
    rank = slots[0].shape[-1]
    vmem = pl.BlockSpec(memory_space=pltpu.VMEM)
    return pl.pallas_call(
        arrange_kernel,
        in_specs=[pl.BlockSpec(memory_space=pltpu.SMEM)] + [vmem] * 4,
        out_specs=vmem,
        out_shape=jax.ShapeDtypeStruct((27 * 24, 6 * rank), BF16),
        scratch_shapes=[pltpu.VMEM((32, 24, rank), F32)],
        compiler_params=limit(6),
        cost_estimate=pl.CostEstimate(flops=0, bytes_accessed=2**21, transcendentals=0),
        name="arrange",
    )(table, *slots)


def final_kernel(scale, factor_ref, first_ref, second_ref, out_ref):
    for i, ref in enumerate((first_ref, second_ref)):
        made = lax.dot_general(ref[...], factor_ref[i], (((1,), (1,)), ((), ())), preferred_element_type=F32)
        out_ref[i] = made * scale


def final(factors, first, second, scale):
    vmem = pl.BlockSpec(memory_space=pltpu.VMEM)
    return pl.pallas_call(
        functools.partial(final_kernel, scale),
        in_specs=[vmem] * 3,
        out_specs=vmem,
        out_shape=jax.ShapeDtypeStruct((2, first.shape[0], first.shape[1] // 6), F32),
        compiler_params=limit(6),
        cost_estimate=pl.CostEstimate(flops=2**29, bytes_accessed=2**22, transcendentals=0),
        name="final",
    )(factors, first, second)


def planes(activations, out_grads, omega):
    layer_count, _, frames, height, widths, channels = activations.shape
    rank = omega.shape[1]
    dp, space = lax.axis_index("dp"), lax.axis_index("space")
    x = space & 1
    me = 8 * dp + space
    core_mask, chip_masks, z_masks = 8, (1, 16, 17), (2, 4, 6)
    table = lax.dynamic_index_in_dim(jnp.asarray(unit_tables()), me, 0, keepdims=False)
    positions = frames * height * widths

    def move(value, mask):
        return swap(value, mask, 32)

    def move_all(values, masks):
        return [move(v, mask) for v, mask in zip(values, masks)]

    acts = activations.reshape(2, positions, channels)
    over = move(acts, core_mask)

    sketched = jnp.dot(out_grads.reshape(-1, channels), omega, preferred_element_type=F32).astype(BF16)
    sketched = sketched.reshape(layer_count, frames, height, widths, rank)
    edge = jnp.where(x == 1, sketched[:, :, height - 1], sketched[:, :, 0])
    pairs = [(i, i + 1) for i in range(1, 7, 2)]
    edge = lax.ppermute(edge, "space", pairs + [(j, i) for i, j in pairs])[:, :, None]
    pieces = pieces_of(table, sketched, edge)

    gram, held = None, []
    for layer in range(2):
        act, *out = turn(table, acts, over, layer, frames)
        got = move_all(out, chip_masks)
        own = [pieces[layer]] + move_all([pieces[layer]] * 3, chip_masks)
        other = [move(piece, core_mask) for piece in own]
        keep, *out = plane(table, act, got, own, other)
        got = move_all(out, z_masks)
        made = gather(table, keep, got, gram)
        gram, (near, far) = made[:-2], made[-2:]
        slots = list(pack(near, move(far, core_mask)))
        slots = slots[:1] + move_all(slots[1:], chip_masks)
        gram = gram[0] if layer == 0 else gram
        held.append(arrange(table, slots))

    mine = gram[0] + move(gram[1], core_mask)
    for masks in (z_masks, chip_masks):
        one, two, both = move_all([mine] * 3, masks)
        mine = (mine + one) + (two + both)
    theirs = move(mine, core_mask)
    factors = inverses_of_factors(table, mine, theirs)
    return final(factors, *held, math.sqrt(27 * channels))


def solution(mesh):
    def body(activations, out_grads, omega):
        fits = (lax.axis_size("dp"), lax.axis_size("space")) == (4, 8)
        fits = fits and activations.shape == (2, 1, 8, 2, 32, 768) and omega.shape[1] == 128
        return (planes if fits else shards)(activations, out_grads, omega)

    return jax.shard_map(
        body,
        mesh=mesh,
        in_specs=(
            P(None, "dp", None, "space", None, None),
            P(None, "dp", None, "space", None, None),
            P(),
        ),
        out_specs=P(None, ("dp", "space"), None),
        check_vma=False,
    )
```
